128 devices in a mesh: section: 2 (over x_lo), expert: 16 (over z, x_hi, core), dp: 4 (over y).
Axes of the slice: x: 4 (x_hi: 2, x_lo: 2; x = x_hi * 2 + x_lo), y: 4, z: 4, core: 2. Of those that a mesh axis runs over, the one named last changes fastest.
Arguments:
- fresh_tokens: bfloat16 [2, 4096, 4096], P(None, ('expert', 'dp')), may hold values from -60 to 60
- in_flight: bfloat16 [4096, 4096], P(('expert', 'dp')), may hold values from -60 to 60
- norm_weight: float32 [2, 4096], P('section'), may hold values from 0.1 to 1.9
- gate_up: bfloat16 [2, 16, 2, 4096, 768], P('section', 'expert', None, 'dp'), may hold values from -0.09375 to 0.09375
- down_proj: bfloat16 [2, 16, 768, 4096], P('section', 'expert', 'dp'), may hold values from -0.21875 to 0.21875
- first_moment: bfloat16 [2, 16, 768, 4096], P('section', 'expert', 'dp'), may hold values from -6 to 6
- second_moment: bfloat16 [2, 16, 768, 4096], P('section', 'expert', 'dp'), may hold values from 0.099609375 to 4
- route_ids: int32 [2, 2, 4096, 8], P('section', None, ('expert', 'dp')), may hold values from 0 to 15, all different within a row; in each aligned block of 64 rows (0 to 63, 64 to 127, ..., all dimensions but the last counted through in order) at most 36 rows name the same one
- route_probs: float32 [2, 2, 4096, 8], P('section', None, ('expert', 'dp')), may hold values from 0.05 to 1
- trade_flags: int32 [8, 1], replicated, may hold values from 0 to 1, as said below
Outputs:
- layer_out: bfloat16 [2, 2, 4096, 4096], P('section', None, ('expert', 'dp'))
- gate_up_moved: bfloat16 [2, 16, 2, 4096, 768], P('section', 'expert', None, 'dp')
- down_moved: bfloat16 [2, 16, 768, 4096], P('section', 'expert', 'dp')
- first_moved: bfloat16 [2, 16, 768, 4096], P('section', 'expert', 'dp')
- second_moved: bfloat16 [2, 16, 768, 4096], P('section', 'expert', 'dp')
The draws below stay inside these ranges and needn't reach their ends.
Inputs may be any that keep to these rules, and one draw needn't show every extreme that they name: `route_ids`: in each aligned block of 64 rows (one device's tokens of one section and tick) the 8 experts of a token differ and no expert is chosen by more than 36 rows. `trade_flags`: at least one entry is 1 and at least one is 0.
All inputs are finite; a program needn't handle non-finite values.
Results may differ from the reference program's by a relative error of at most 0.0035.
Values may be sent and summed in bfloat16 or wider, within the bound.
A program may use at most 128 MiB of HBM per device.

```python
import math
import jax
import jax.numpy as jnp
import numpy as np
from jax import lax

D = 4096
FF = 768
EXPERTS = 16
TOPK = 8
TICKS = 2
TOK_DEV = 64
SECTIONS = 2
EXP_DEV = 1
CAP = 36
TOKENS = 4096
PAIRS = 8
N_EXPERT = 16
N_DP = 4


def scaled_rows(key, shape):
    key_value, key_row, key_col = jax.random.split(key, 3)
    values = jax.random.normal(key_value, shape, jnp.float32)
    row_scale = jnp.exp(jax.random.uniform(key_row, shape[:-1] + (1,), jnp.float32, -1.15, 1.15))
    col_scale = jnp.exp(jax.random.uniform(key_col, (shape[-1],), jnp.float32, -1.15, 1.15))
    return jnp.clip(values * row_scale * col_scale, -60.0, 60.0)


def draw_fresh_tokens(key, part):
    return scaled_rows(jax.random.fold_in(key, 11), (TICKS, TOKENS, D)).astype(jnp.bfloat16)


def draw_in_flight(key, part):
    return scaled_rows(jax.random.fold_in(key, 23), (TOKENS, D)).astype(jnp.bfloat16)


def draw_trade_flags(key, part):
    key_perm, key_count = jax.random.split(jax.random.fold_in(key, 37))
    entries = PAIRS * EXP_DEV
    ordering = jax.random.permutation(key_perm, entries)
    how_many = jax.random.randint(key_count, (), 1, entries)
    return (ordering < how_many).astype(jnp.int32).reshape(PAIRS, EXP_DEV)


def block_levels(own_key, extent, cuts, low, top_value):
    def one(position, parts):
        steps = jax.random.uniform(jax.random.fold_in(jax.random.fold_in(own_key, 6), position), (parts,), jnp.float32, low / len(cuts), top_value / len(cuts))
        return jnp.repeat(jnp.exp(steps), extent[position] // parts).reshape((-1,) + (1,) * (len(extent) - position - 1))

    factor_of = one(*cuts[0])
    for cut in cuts[1:]:
        factor_of = factor_of * one(*cut)
    return factor_of


def deal_out(own_key, own, number, rows, amount, top, bound, skew):
    ranking = jax.random.permutation(own_key, amount)
    crowded, ordinary = portions_of(amount, rows * top, bound, skew, True), portions_of(amount, rows * top, bound, skew, False)
    places = jnp.arange(amount)

    def named(sizes, offset_by):
        used = int((sizes > 0).sum())
        fixed = max(1, used // 4)
        moved = fixed + (places - fixed + offset_by * (used - fixed)) % max(1, amount - fixed)
        return jnp.zeros((amount,), jnp.int32).at[ranking[jnp.where(places < fixed, places, moved)]].set(jnp.asarray(sizes, jnp.int32))

    sizes = jnp.where(number % 4 == 0, named(crowded, number // 4), named(ordinary, number - number // 4 - 1))
    mixed = jax.random.permutation(jax.random.fold_in(own, 3), amount)
    source_of, sink = mixed[0:amount // 2 * 2:2], mixed[1:amount // 2 * 2:2]
    room = jnp.minimum(sizes[source_of] - 1, bound - sizes[sink]) // 2
    room = jnp.where((source_of == ranking[0]) | (sink == ranking[0]) | (sizes[sink] == 0), 0, jnp.maximum(room, 0))
    moved = jax.random.randint(jax.random.fold_in(own, 4), (amount // 2,), 0, 1 << 20) % (room + 1)
    sizes = sizes.at[source_of].add(-moved).at[sink].add(moved)
    labels = jnp.searchsorted(jnp.cumsum(sizes), jnp.arange(rows * top), side="right").astype(jnp.int32)
    grid = labels.reshape(top, rows).T
    grid = grid[jax.random.permutation(jax.random.fold_in(own, 1), rows)]
    offset_by = jax.random.randint(jax.random.fold_in(own, 2), (rows, 1), 0, top)
    return jnp.take_along_axis(grid, (jnp.arange(top)[None, :] + offset_by) % top, axis=1)


def portions_of(count, total, most, slope, full):
    portions = [(1 << 20) // math.isqrt(grade ** slope) + 1 for grade in range(1, count + 1)]
    largest = most if full else min(most, max(-(-total // count), total * portions[0] // sum(portions)))
    least = 1 if total - largest >= count - 1 else 0
    given, rest = [largest] + [least] * (count - 1), total - largest - least * (count - 1)
    while rest > 0:
        movable = [i for i in range(1, count) if given[i] < largest] or [i for i in range(1, count) if given[i] < most]
        pool, budget = sum([portions[i] for i in movable]), rest
        for i in movable:
            addition = min(most - given[i], max(1, budget * portions[i] // pool), rest)
            given[i] = given[i] + addition
            rest = rest - addition
    return np.array(given)


def centred(rng, extent, spread, limit, cuts=(), kind=jnp.bfloat16):
    values = spread * jax.random.normal(rng, extent, jnp.float32)
    if cuts:
        values = values * block_levels(rng, extent, cuts, -0.22, 0.18)
    return jnp.clip(values, -limit, limit).astype(kind)


def setup_inputs(seed: int = 0) -> dict:
    seeds = jax.random.split(jax.random.key(seed), 11)
    fresh_tokens = draw_fresh_tokens(jax.random.fold_in(seeds[10], 71), 0)
    in_flight = draw_in_flight(jax.random.fold_in(seeds[10], 71), 0)
    norm_weight = jnp.clip(1.0 + 0.18 * jax.random.normal(seeds[2], (SECTIONS, D), jnp.float32), 0.1, 1.9)
    gate_up = centred(seeds[3], (SECTIONS, EXPERTS, 2, D, FF), D ** -0.5, 0.09375, ((0, 2), (1, 16), (3, 4)))
    down_proj = centred(seeds[4], (SECTIONS, EXPERTS, FF, D), FF ** -0.5, 0.21875, ((0, 2), (1, 16), (2, 4)))
    first_moment = centred(seeds[5], (SECTIONS, EXPERTS, FF, D), 1.0, 6.0, ((0, 2), (1, 16), (2, 4)))
    second_moment = jnp.clip(jnp.exp(math.log(4.0) - 3.6927934 * jax.random.uniform(seeds[6], (SECTIONS, EXPERTS, FF, D), jnp.float32) ** block_levels(seeds[6], (SECTIONS, EXPERTS, FF, D), ((0, 2), (1, 16), (2, 4)), -0.2, 0.2)), 0.099609375, 4.0).astype(jnp.bfloat16)
    route_ids_keys = jax.random.split(jax.random.fold_in(seeds[7], 1), SECTIONS * TICKS * TOKENS // TOK_DEV)
    route_ids_turns = jax.random.permutation(jax.random.fold_in(seeds[7], 3), SECTIONS * TICKS * TOKENS // TOK_DEV)
    route_ids = jax.vmap(lambda own, number: deal_out(jax.random.fold_in(seeds[7], 2), own, number, TOK_DEV, EXPERTS, TOPK, CAP, 2))(route_ids_keys, route_ids_turns).reshape((SECTIONS, TICKS, TOKENS, TOPK))
    route_probs = jnp.clip(jnp.exp(math.log(1.0) - 2.9957323 * jax.random.uniform(seeds[8], (SECTIONS, TICKS, TOKENS, TOPK), jnp.float32) ** block_levels(seeds[8], (SECTIONS, TICKS, TOKENS, TOPK), ((0, 2), (2, 64)), -0.2, 0.2)), 0.05, 1.0)
    trade_flags = draw_trade_flags(jax.random.fold_in(seeds[10], 71), 0)
    return dict(fresh_tokens=fresh_tokens, in_flight=in_flight, norm_weight=norm_weight, gate_up=gate_up, down_proj=down_proj, first_moment=first_moment, second_moment=second_moment, route_ids=route_ids, route_probs=route_probs, trade_flags=trade_flags)


def rms_normed(inputs, norm_gain):
    values = inputs.astype(jnp.float32)
    inverse_rms = lax.rsqrt(lax.optimization_barrier(jnp.mean(values * values, axis=-1, keepdims=True)) + 1e-06)
    return (values * inverse_rms * norm_gain).astype(jnp.bfloat16)

def moe_layer(inputs, norm_gain, section_gate_up, section_down, layer_ids, layer_probs):
    normed = rms_normed(inputs, norm_gain)
    mix_weight = layer_probs / lax.optimization_barrier(jnp.sum(layer_probs, axis=-1, keepdims=True))
    flat_ids = layer_ids.reshape(-1)
    flat_weight = mix_weight.reshape(-1)
    most_rows = N_EXPERT * N_DP * CAP
    token_count = normed.shape[0]

    def per_expert(running, expert):
        member = (flat_ids != expert).astype(jnp.int32)
        ordering = jnp.argsort(member, stable=True)[:most_rows].astype(jnp.int32)
        live_rows = member[ordering] == 0
        token_rows = (ordering // TOPK).astype(jnp.int32)
        rows_in = normed[token_rows]
        gate_part = jnp.dot(rows_in, section_gate_up[expert, 0], preferred_element_type=jnp.float32)
        up_part = jnp.dot(rows_in, section_gate_up[expert, 1], preferred_element_type=jnp.float32)
        active = (jax.nn.silu(gate_part) * up_part).astype(jnp.bfloat16)
        expert_out = jnp.dot(active, section_down[expert], preferred_element_type=jnp.float32).astype(jnp.bfloat16)
        scaled = jnp.where(live_rows, flat_weight[ordering], 0.0)[:, None] * expert_out.astype(jnp.float32)
        running = running + jax.ops.segment_sum(scaled, token_rows, num_segments=token_count)
        return (running, None)
    running, _ = lax.scan(per_expert, inputs.astype(jnp.float32), jnp.arange(EXPERTS, dtype=jnp.int32))
    return running.astype(jnp.bfloat16)

def reference(fresh_tokens, in_flight, norm_weight, gate_up, down_proj, first_moment, second_moment, route_ids, route_probs, trade_flags):
    section_rows = []
    for section_step in range(SECTIONS):
        tick_list = []
        for tick_step in range(TICKS):
            if section_step == 0:
                inputs = fresh_tokens[tick_step]
            elif tick_step == 0:
                inputs = in_flight
            else:
                inputs = section_rows[section_step - 1][tick_step - 1]
            tick_list.append(moe_layer(inputs, norm_weight[section_step], gate_up[section_step], down_proj[section_step], route_ids[section_step, tick_step], route_probs[section_step, tick_step]))
        section_rows.append(tick_list)
    layer_out = jnp.stack([jnp.stack(tick_list) for tick_list in section_rows])
    half_span = N_EXPERT // 2
    per_device = EXPERTS // N_EXPERT
    blocks = jnp.arange(N_EXPERT, dtype=jnp.int32)
    pair_flags = trade_flags[blocks % half_span]
    source = jnp.where(pair_flags == 1, (blocks ^ half_span)[:, None], blocks[:, None]).astype(jnp.int32)
    slot_grid = jnp.broadcast_to(jnp.arange(per_device, dtype=jnp.int32)[None, :], (N_EXPERT, per_device))

    def relocate(stacked):
        shaped = stacked.reshape((SECTIONS, N_EXPERT, per_device) + stacked.shape[2:])
        return shaped[:, source, slot_grid].reshape(stacked.shape)
    return (layer_out, relocate(gate_up), relocate(down_proj), relocate(first_moment), relocate(second_moment))
```

```python
import jax
import jax.numpy as jnp
from jax import lax
from jax.sharding import PartitionSpec as P

EXPERTS = 16


def partner(value, axis, bit):
    return lax.ppermute(value, axis, [(i, i ^ 1 << bit) for i in range(lax.axis_size(axis))])


def shifted(block, axis, distance):
    devices = range(lax.axis_size(axis))
    route = [(i - distance, i) for i in devices if i - distance in devices]
    return lax.ppermute(block, axis, route)


def rms_normed(inputs, norm_gain):
    values = inputs.astype(jnp.float32)
    inverse_rms = lax.rsqrt(jnp.mean(values * values, axis=-1, keepdims=True) + 1e-06)
    return (values * inverse_rms * norm_gain).astype(jnp.bfloat16)


def per_device(
    fresh_tokens,
    in_flight,
    norm_weight,
    gate_up,
    down_proj,
    first_moment,
    second_moment,
    route_ids,
    route_probs,
    trade_flags,
):
    groups = lax.axis_size("expert")
    half_span = groups // 2
    top_bit = groups.bit_length() - 2
    own_rank = lax.axis_index("expert")
    section_index = lax.axis_index("section")
    full_gate_up = lax.all_gather(gate_up, "dp", axis=3, tiled=True)
    full_down = lax.all_gather(down_proj, "dp", axis=2, tiled=True)
    gate_weights = full_gate_up[0, 0, 0]
    up_weights = full_gate_up[0, 0, 1]
    down_weights = full_down[0, 0]
    expert_ids = jnp.arange(EXPERTS, dtype=jnp.int32)
    probs = route_probs[0]
    mix = probs / jnp.sum(probs, axis=-1, keepdims=True)
    chosen = route_ids[0][:, :, :, None] == expert_ids
    dense_mix = jnp.sum(jnp.where(chosen, mix[:, :, :, None], 0.0), axis=2)
    all_mix = lax.all_gather(dense_mix, "expert", axis=1, tiled=True)
    own_mix = jnp.sum(jnp.where(expert_ids == own_rank, all_mix, 0.0), axis=-1)

    traded = partner((gate_up, down_proj, first_moment, second_moment), "expert", top_bit)

    def layer(inputs, scale, held=None):
        normed = rms_normed(inputs, norm_weight[0])
        arrived = lax.all_gather(normed, "expert", axis=0, tiled=True)
        gate_part = jnp.dot(arrived, gate_weights, preferred_element_type=jnp.float32)
        up_part = jnp.dot(arrived, up_weights, preferred_element_type=jnp.float32)
        active = (jax.nn.silu(gate_part) * up_part).astype(jnp.bfloat16)
        result = jnp.dot(active, down_weights, preferred_element_type=jnp.float32)
        result = (result * scale[:, None]).astype(jnp.bfloat16)
        if held is not None:
            result, held = lax.optimization_barrier((result, held))
        combined = lax.psum_scatter(result, "expert", scatter_dimension=0, tiled=True)
        return (inputs.astype(jnp.float32) + combined.astype(jnp.float32)).astype(jnp.bfloat16), held

    first_input = jnp.where(section_index == 0, fresh_tokens[0], in_flight)
    tick_zero, traded = layer(first_input, own_mix[0], traded)
    arrived = shifted(tick_zero, "section", 1)
    second_input = jnp.where(section_index == 0, fresh_tokens[1], arrived)
    tick_one, _ = layer(second_input, own_mix[1])
    layer_out = jnp.stack([tick_zero, tick_one])[None]

    own_flags = trade_flags[own_rank % half_span] == 1
    mask_five = own_flags[None, :, None, None, None]
    mask_four = own_flags[None, :, None, None]
    gate_up_moved = jnp.where(mask_five, traded[0], gate_up)
    down_moved = jnp.where(mask_four, traded[1], down_proj)
    first_moved = jnp.where(mask_four, traded[2], first_moment)
    second_moved = jnp.where(mask_four, traded[3], second_moment)
    return (layer_out, gate_up_moved, down_moved, first_moved, second_moved)


def solution(mesh):
    return jax.shard_map(
        per_device,
        mesh=mesh,
        in_specs=(
            P(None, ("expert", "dp"), None),
            P(("expert", "dp"), None),
            P("section", None),
            P("section", "expert", None, "dp", None),
            P("section", "expert", "dp", None),
            P("section", "expert", "dp", None),
            P("section", "expert", "dp", None),
            P("section", None, ("expert", "dp"), None),
            P("section", None, ("expert", "dp"), None),
            P(),
        ),
        out_specs=(
            P("section", None, ("expert", "dp"), None),
            P("section", "expert", None, "dp", None),
            P("section", "expert", "dp", None),
            P("section", "expert", "dp", None),
            P("section", "expert", "dp", None),
        ),
        check_vma=False,
    )
```

```python
import jax
import jax.numpy as jnp
from jax import lax
from jax.experimental import pallas as pl
from jax.experimental.pallas import tpu as pltpu
from jax.sharding import PartitionSpec as P

EXPERTS = 16
MESH = pl.DeviceIdType.MESH
ANY = pl.BlockSpec(memory_space=pl.ANY)
VMEM = pl.BlockSpec(memory_space=pltpu.VMEM)
DMA = pltpu.SemaphoreType.DMA
CHIPS = [(dz, dx) for dz in (1, 3, 2, 0) for dx in (0, 1) if dz or dx]


def chip_peer(rank, dz, dx):
    return lax.rem(rank + 4 * dz, EXPERTS) ^ (2 * dx)


def remote(src, dst, send_sem, recv_sem, **device):
    return pltpu.make_async_remote_copy(
        src_ref=src,
        dst_ref=dst,
        send_sem=send_sem,
        recv_sem=recv_sem,
        device_id=device,
        device_id_type=MESH,
    )


def greet(devices):
    barrier = pltpu.get_barrier_semaphore()
    for device in devices:
        pl.semaphore_signal(barrier, inc=1, device_id=device, device_id_type=MESH)
    pl.semaphore_wait(barrier, len(devices))


def block(ref, rank, rows):
    return ref.at[pl.ds(pl.multiple_of(rank * rows, rows), rows)]


def gather_start(pairs, sems, rank):
    send, recv = sems
    local, first = [], []
    for k, (own, whole) in enumerate(pairs):
        rows = own.shape[0]
        here = pltpu.make_async_copy(own, block(whole, rank, rows), send.at[k, 15])
        here.start()
        local.append(here)
        for i, (dz, dx) in enumerate(CHIPS):
            copy = remote(
                own, block(whole, rank, rows), send.at[k, i], recv.at[k, i],
                expert=chip_peer(rank, dz, dx),
            )
            copy.start()
            first.append(copy)
        copy = remote(own, block(whole, rank, rows), send.at[k, 14], recv.at[k, 14], expert=rank ^ 1)
        copy.start()
        first.append(copy)
    return local, first


def gather_finish(pairs, sems, rank, started):
    send, recv = sems
    local, first = started
    second = []
    for i, (dz, dx) in enumerate(CHIPS):
        source = chip_peer(rank, (4 - dz) % 4, dx)
        for k, (own, whole) in enumerate(pairs):
            rows = own.shape[0]
            first[k * 8 + i].wait_recv()
            landed = block(whole, source, rows)
            copy = remote(landed, landed, send.at[k, 7 + i], recv.at[k, 7 + i], expert=rank ^ 1)
            copy.start()
            second.append(copy)
    for k in range(len(pairs)):
        first[k * 8 + 7].wait_recv()
    for copy in second:
        copy.wait_recv()
    for copy in first + second:
        copy.wait_send()
    for copy in local:
        copy.wait()


def group(rank):
    return [{"expert": chip_peer(rank, dz, dx)} for dz, dx in CHIPS] + [{"expert": rank ^ 1}]


def weights_kernel(gate_up, down, tokens, mix, full_gate_up, full_down, all_tokens, all_mix,
                   send, recv, here, token_send, token_recv):
    rank, place = lax.axis_index("expert"), lax.axis_index("dp")
    right, left = lax.rem(place + 1, 4), lax.rem(place + 3, 4)
    greet([{"dp": right}, {"dp": left}] + group(rank))
    deep, low = gate_up.shape[1], down.shape[0]
    half = low // 2

    def gate_part(k, owner):
        return full_gate_up.at[k, pl.ds(pl.multiple_of(owner * deep, deep), deep)]

    def down_part(k, owner):
        return full_down.at[pl.ds(pl.multiple_of(owner * low + k * half, half), half)]

    own = [gate_up.at[0], gate_up.at[1], down.at[pl.ds(0, half)], down.at[pl.ds(half, half)]]
    parts = [lambda o: gate_part(0, o), lambda o: gate_part(1, o),
             lambda o: down_part(0, o), lambda o: down_part(1, o)]
    copies = []
    for k in range(4):
        copies.append((
            remote(own[k], parts[k](place), send.at[k, 0], recv.at[k, 0], dp=right),
            remote(own[k], parts[k](place), send.at[k, 1], recv.at[k, 1], dp=left),
        ))
    for k in (0, 2):
        copies[k][0].start()
        copies[k + 1][1].start()
    for k in (0, 2):
        copies[k + 1][0].start()
        copies[k][1].start()
    pairs = [(tokens, all_tokens), (mix, all_mix)]
    sems = (token_send, token_recv)
    started = gather_start(pairs, sems, rank)
    local = []
    for k in range(4):
        copy = pltpu.make_async_copy(own[k], parts[k](place), here.at[k])
        copy.start()
        local.append(copy)
    passed = []
    for k in range(4):
        way = k % 2
        owner, device = ((left, right), (right, left))[way]
        copies[k][way].wait_recv()
        copy = remote(parts[k](owner), parts[k](owner), send.at[k, 2], recv.at[k, 2], dp=device)
        copy.start()
        passed.append(copy)
    gather_finish(pairs, sems, rank, started)
    for k in range(4):
        copies[k][1 - k % 2].wait_recv()
        passed[k].wait_recv()
    for k in range(4):
        copies[k][0].wait_send()
        copies[k][1].wait_send()
        passed[k].wait_send()
        local[k].wait()


def gather_weights(gate_up, down, tokens, mix):
    width = tokens.shape[1]
    return pl.pallas_call(
        weights_kernel,
        out_shape=(
            jax.ShapeDtypeStruct((2, 4 * gate_up.shape[1], gate_up.shape[2]), jnp.bfloat16),
            jax.ShapeDtypeStruct((4 * down.shape[0], width), jnp.bfloat16),
            jax.ShapeDtypeStruct((EXPERTS * tokens.shape[0], width), jnp.bfloat16),
            jax.ShapeDtypeStruct((EXPERTS * mix.shape[0], mix.shape[1]), jnp.float32),
        ),
        in_specs=[ANY] * 4,
        out_specs=[ANY] * 4,
        scratch_shapes=[
            DMA((4, 3)), DMA((4, 3)), DMA((4,)), DMA((2, 16)), DMA((2, 16)),
        ],
        compiler_params=pltpu.CompilerParams(collective_id=0, has_side_effects=True),
        name="gather_weights",
    )(gate_up, down, tokens, mix)


def tokens_kernel(tokens, all_tokens, token_send, token_recv):
    rank = lax.axis_index("expert")
    greet(group(rank))
    pairs, sems = [(tokens, all_tokens)], (token_send, token_recv)
    gather_finish(pairs, sems, rank, gather_start(pairs, sems, rank))


def gather_tokens(tokens):
    return pl.pallas_call(
        tokens_kernel,
        out_shape=jax.ShapeDtypeStruct((EXPERTS * tokens.shape[0], tokens.shape[1]), jnp.bfloat16),
        in_specs=[ANY],
        out_specs=ANY,
        scratch_shapes=[DMA((1, 16)), DMA((1, 16))],
        compiler_params=pltpu.CompilerParams(collective_id=1, has_side_effects=True),
        name="gather_tokens",
    )(tokens)


def combine_kernel(partial, inputs, out, mine, theirs, summed, arrived, sib_send, sib_recv,
                   load, send, recv):
    rank = lax.axis_index("expert")
    rows, width = inputs.shape
    greet(group(rank))
    steps = CHIPS + [(0, 0)]
    sibling = []
    for i, (dz, dx) in enumerate(steps):
        home = chip_peer(rank, dz, dx)
        copy = remote(block(partial, home ^ 1, rows), theirs.at[i], sib_send.at[i], sib_recv.at[i],
                      expert=rank ^ 1)
        copy.start()
        sibling.append(copy)
    loads = []
    for i, (dz, dx) in enumerate(steps):
        copy = pltpu.make_async_copy(block(partial, chip_peer(rank, dz, dx), rows), mine.at[i], load.at[i])
        copy.start()
        loads.append(copy)
    copies = []
    for i, (dz, dx) in enumerate(steps):
        loads[i].wait()
        sibling[i].wait_recv()

        @pl.loop(0, rows // 16)
        def _(r):
            part = pl.ds(pl.multiple_of(r * 16, 16), 16)
            total = mine[i, part, :].astype(jnp.float32) + theirs[i, part, :].astype(jnp.float32)
            summed[i, part, :] = total.astype(jnp.bfloat16)

        if i < 7:
            copy = remote(summed.at[i], arrived.at[i], send.at[i], recv.at[i],
                          expert=chip_peer(rank, dz, dx))
            copy.start()
            copies.append(copy)
    for copy in copies:
        copy.wait_recv()

    @pl.loop(0, rows // 16)
    def _(r):
        part = pl.ds(pl.multiple_of(r * 16, 16), 16)
        total = inputs[part, :].astype(jnp.float32) + summed[7, part, :].astype(jnp.float32)
        for i in range(7):
            total = total + arrived[i, part, :].astype(jnp.float32)
        out[part, :] = total.astype(jnp.bfloat16)

    for copy in copies + sibling:
        copy.wait_send()


def combine(partial, inputs):
    rows, width = inputs.shape
    slot = pltpu.VMEM((8, rows, width), jnp.bfloat16)
    return pl.pallas_call(
        combine_kernel,
        out_shape=jax.ShapeDtypeStruct(inputs.shape, jnp.bfloat16),
        in_specs=[ANY, VMEM],
        out_specs=VMEM,
        scratch_shapes=[
            slot, slot, slot, pltpu.VMEM((7, rows, width), jnp.bfloat16),
            DMA((8,)), DMA((8,)), DMA((8,)), DMA((7,)), DMA((7,)),
        ],
        compiler_params=pltpu.CompilerParams(
            collective_id=2, has_side_effects=True, vmem_limit_bytes=40 << 20
        ),
        name="combine",
    )(partial, inputs)


def partner(value, axis, bit):
    return lax.ppermute(value, axis, [(i, i ^ 1 << bit) for i in range(lax.axis_size(axis))])


def shifted(value, axis, distance):
    devices = range(lax.axis_size(axis))
    route = [(i - distance, i) for i in devices if i - distance in devices]
    return lax.ppermute(value, axis, route)


def rms_normed(inputs, norm_gain):
    values = inputs.astype(jnp.float32)
    inverse_rms = lax.rsqrt(jnp.mean(values * values, axis=-1, keepdims=True) + 1e-06)
    return (values * inverse_rms * norm_gain).astype(jnp.bfloat16)


def expert_ffn(rows_in, gate_up, down, scale):
    gate_part = jnp.dot(rows_in, gate_up[0], preferred_element_type=jnp.float32)
    up_part = jnp.dot(rows_in, gate_up[1], preferred_element_type=jnp.float32)
    active = (jax.nn.silu(gate_part) * up_part).astype(jnp.bfloat16)
    result = jnp.dot(active, down, preferred_element_type=jnp.float32)
    return (result * scale[:, None]).astype(jnp.bfloat16)


def per_device(
    fresh_tokens,
    in_flight,
    norm_weight,
    gate_up,
    down_proj,
    first_moment,
    second_moment,
    route_ids,
    route_probs,
    trade_flags,
):
    groups = lax.axis_size("expert")
    half_span = groups // 2
    top_bit = groups.bit_length() - 2
    own_rank = lax.axis_index("expert")
    section_index = lax.axis_index("section")
    traded = partner((gate_up, down_proj, first_moment, second_moment), "expert", top_bit)

    lanes = jnp.arange(128, dtype=jnp.int32)
    probs = route_probs[0]
    mix = probs / jnp.sum(probs, axis=-1, keepdims=True)
    wanted = route_ids[0] + EXPERTS * jnp.arange(2, dtype=jnp.int32)[:, None, None]
    dense_mix = jnp.sum(jnp.where(wanted[..., None] == lanes, mix[..., None], 0.0), axis=(0, 2))

    first_input = jnp.where(section_index == 0, fresh_tokens[0], in_flight)
    full_gate_up, full_down, all_tokens, all_mix = gather_weights(
        gate_up[0, 0], down_proj[0, 0], rms_normed(first_input, norm_weight[0]), dense_mix
    )

    def own_mix(tick):
        return jnp.sum(jnp.where(lanes == tick * EXPERTS + own_rank, all_mix, 0.0), axis=-1)

    partial = expert_ffn(all_tokens, full_gate_up, full_down, own_mix(0))
    partial, traded = lax.optimization_barrier((partial, traded))
    tick_zero = combine(partial, first_input)
    arrived = shifted(tick_zero, "section", 1)
    second_input = jnp.where(section_index == 0, fresh_tokens[1], arrived)
    all_tokens = gather_tokens(rms_normed(second_input, norm_weight[0]))
    partial = expert_ffn(all_tokens, full_gate_up, full_down, own_mix(1))
    tick_one = combine(partial, second_input)
    layer_out = jnp.stack([tick_zero, tick_one])[None]

    own_flags = trade_flags[own_rank % half_span] == 1
    mask_five = own_flags[None, :, None, None, None]
    mask_four = own_flags[None, :, None, None]
    gate_up_moved = jnp.where(mask_five, traded[0], gate_up)
    down_moved = jnp.where(mask_four, traded[1], down_proj)
    first_moved = jnp.where(mask_four, traded[2], first_moment)
    second_moved = jnp.where(mask_four, traded[3], second_moment)
    return (layer_out, gate_up_moved, down_moved, first_moved, second_moved)


def solution(mesh):
    return jax.shard_map(
        per_device,
        mesh=mesh,
        in_specs=(
            P(None, ("expert", "dp"), None),
            P(("expert", "dp"), None),
            P("section", None),
            P("section", "expert", None, "dp", None),
            P("section", "expert", "dp", None),
            P("section", "expert", "dp", None),
            P("section", "expert", "dp", None),
            P("section", None, ("expert", "dp"), None),
            P("section", None, ("expert", "dp"), None),
            P(),
        ),
        out_specs=(
            P("section", None, ("expert", "dp"), None),
            P("section", "expert", None, "dp", None),
            P("section", "expert", "dp", None),
            P("section", "expert", "dp", None),
            P("section", "expert", "dp", None),
        ),
        check_vma=False,
    )
```

```python
import functools

import jax
import jax.numpy as jnp
from jax import lax
from jax.experimental import pallas as pl
from jax.experimental.pallas import tpu as pltpu
from jax.sharding import PartitionSpec as P

EXPERTS = 16
BLOCK = 64
PLANE = 4 * BLOCK
TILE = 256
MESH = pl.DeviceIdType.MESH
ANY = pl.BlockSpec(memory_space=pl.ANY)
VMEM = pl.BlockSpec(memory_space=pltpu.VMEM)
DMA = pltpu.SemaphoreType.DMA
STEPS = (1, 3, 2)
HOMES = (0, 3, 1, 2)


def along_z(rank, step):
    return lax.rem(rank + 4 * step, EXPERTS)


def remote(src, dst, sems, device):
    return pltpu.make_async_remote_copy(
        src_ref=src,
        dst_ref=dst,
        send_sem=sems[0],
        recv_sem=sems[1],
        device_id=device,
        device_id_type=MESH,
    )


def greet(devices):
    barrier = pltpu.get_barrier_semaphore()
    for device in devices:
        pl.semaphore_signal(barrier, inc=1, device_id=device, device_id_type=MESH)
    pl.semaphore_wait(barrier, len(devices))


def group(rank):
    return [{"expert": along_z(rank, step)} for step in STEPS] + [
        {"expert": rank ^ 2},
        {"expert": rank ^ 1},
    ]


def over_tiles(low, high, body):
    @pl.loop(0, BLOCK // 16)
    def _(r):
        rows = pl.ds(pl.multiple_of(r * 16, 16), 16)

        @pl.loop(low // 512, high // 512)
        def _(c):
            body(rows, pl.ds(pl.multiple_of(c * 512, 512), 512))


class Spread:
    def __init__(self, whole, cut, sems, rank):
        self.whole, self.cut, self.rank = whole, cut, rank
        self.width = whole.shape[1]
        self.sems = sems
        self.sources = [along_z(rank, 4 - step) for step in STEPS]
        self.sent = []
        own = self.at(rank)
        self.first = [
            self.copy(own, i, {"expert": along_z(rank, step)}) for i, step in enumerate(STEPS)
        ]
        self.first.append(self.copy(own, 3, {"expert": rank ^ 2}))
        self.first.append(self.copy(own, 4, {"expert": rank ^ 1}))
        self.over_x, self.over_z, self.siblings = [], [], {}

    def at(self, owner, low=0, high=None):
        rows = pl.ds(pl.multiple_of(owner * BLOCK, BLOCK), BLOCK)
        if low == 0 and high is None:
            return self.whole.at[rows]
        return self.whole.at[rows, pl.ds(low, high - low)]

    def copy(self, ref, i, device):
        return remote(ref, ref, (self.sems[0].at[i], self.sems[1].at[i]), device)

    def start(self, copy):
        copy.start()
        self.sent.append(copy)
        return copy

    def begin(self):
        for copy in self.first:
            self.start(copy)

    def to_sibling(self, key, owner, i):
        self.siblings[key] = self.start(self.copy(self.at(owner), i, {"expert": self.rank ^ 1}))

    def forward_x_arrival(self):
        self.first[3].wait_recv()
        if self.cut < self.width:
            for i, step in enumerate(STEPS):
                ref = self.at(self.rank ^ 2, self.cut, self.width)
                self.over_z.append(
                    self.start(self.copy(ref, 8 + i, {"expert": along_z(self.rank, step)}))
                )
        self.to_sibling("x", self.rank ^ 2, 11)

    def forward_z_arrival(self, i):
        self.first[i].wait_recv()
        high = None if self.cut == self.width else self.cut
        self.over_x.append(
            self.start(self.copy(self.at(self.sources[i], 0, high), 5 + i, {"expert": self.rank ^ 2}))
        )
        self.to_sibling(("z", i), self.sources[i], 12 + i)

    def forward_far_arrival(self, i):
        self.over_x[i].wait_recv()
        if self.over_z:
            self.over_z[i].wait_recv()
        self.to_sibling(("far", i), self.sources[i] ^ 2, 15 + i)

    def wait_own_plane(self):
        self.first[4].wait_recv()
        self.siblings["x"].wait_recv()

    def wait_plane(self, i):
        self.siblings[("z", i)].wait_recv()
        self.siblings[("far", i)].wait_recv()

    def finish(self):
        for copy in self.sent:
            copy.wait_send()


class Combine:
    def __init__(self, partial, theirs, over_x, from_z, halves, last, cut, sems, rank):
        self.partial, self.theirs, self.over_x, self.from_z = partial, theirs, over_x, from_z
        self.halves, self.last, self.cut, self.rank = halves, last, cut, rank
        self.width = partial.shape[2]
        self.send, self.recv = sems
        self.side = lax.rem(rank // 2, 2)
        self.core = lax.rem(rank, 2)
        self.sent = []
        self.sibling, self.x_copies, self.z_copies, self.half_copies = {}, {}, {}, {}

    def start(self, src, dst, i, device):
        copy = remote(src, dst, (self.send.at[i], self.recv.at[i]), {"expert": device})
        copy.start()
        self.sent.append(copy)
        return copy

    def rows(self, dx, core):
        side = self.side if dx == 0 else 1 - self.side
        return pl.multiple_of((side * 2 + core) * BLOCK, BLOCK)

    def to_sibling(self, m):
        for dx in (1, 0):
            src = self.partial.at[m, pl.ds(self.rows(dx, 1 - self.core), BLOCK)]
            self.sibling[m, dx] = self.start(src, self.theirs.at[m, dx], 2 * m + dx, self.rank ^ 1)

    def add_sibling(self, m):
        peer = along_z(self.rank, HOMES[m])
        for dx in (1, 0):
            self.sibling[m, dx].wait_recv()
            base = self.rows(dx, self.core)

            def body(rows, columns):
                mine = self.partial[m, pl.ds(pl.multiple_of(base + rows.start, 16), 16), columns]
                total = mine.astype(jnp.float32) + self.theirs[m, dx, rows, columns].astype(jnp.float32)
                self.theirs[m, dx, rows, columns] = total.astype(jnp.bfloat16)

            over_tiles(0, self.width, body)
            if dx == 1:
                below = pl.ds(0, self.cut)
                self.x_copies[m] = self.start(
                    self.theirs.at[m, 1, :, below], self.over_x.at[m, :, below], 8 + m, self.rank ^ 2
                )
            if self.cut < self.width and m:
                above = pl.ds(self.cut, self.width - self.cut)
                self.half_copies[m, dx] = self.start(
                    self.theirs.at[m, dx, :, above], self.halves.at[m - 1, dx], 12 + 2 * m + dx, peer
                )

    def add_x(self, m):
        self.x_copies[m].wait_recv()

        def body(rows, columns):
            total = self.over_x[m, rows, columns].astype(jnp.float32)
            total = total + self.theirs[m, 0, rows, columns].astype(jnp.float32)
            self.over_x[m, rows, columns] = total.astype(jnp.bfloat16)

        over_tiles(0, self.cut, body)
        if m:
            below = pl.ds(0, self.cut)
            self.z_copies[m] = self.start(
                self.over_x.at[m, :, below], self.from_z.at[m - 1, :, below], 20 + m,
                along_z(self.rank, HOMES[m]),
            )

    def finish(self, inputs, out):
        cut, width = self.cut, self.width
        if cut < width:
            for m in (1, 2, 3):
                for dx in (1, 0):
                    self.half_copies[m, dx].wait_recv()

            def gathered(dx, rows, columns):
                total = self.theirs[0, dx, rows, columns].astype(jnp.float32)
                inner = pl.ds(pl.multiple_of(columns.start - cut, 512), 512)
                for m in range(3):
                    total = total + self.halves[m, dx, rows, inner].astype(jnp.float32)
                return total

            def other(rows, columns):
                self.theirs[0, 1, rows, columns] = gathered(1, rows, columns).astype(jnp.bfloat16)

            over_tiles(cut, width, other)
            above = pl.ds(cut, width - cut)
            copy = self.start(self.theirs.at[0, 1, :, above], self.last, 24, self.rank ^ 2)

        for m in (1, 2, 3):
            self.z_copies[m].wait_recv()

        def near(rows, columns):
            total = inputs[rows, columns].astype(jnp.float32)
            total = total + self.over_x[0, rows, columns].astype(jnp.float32)
            for m in range(3):
                total = total + self.from_z[m, rows, columns].astype(jnp.float32)
            out[rows, columns] = total.astype(jnp.bfloat16)

        over_tiles(0, cut, near)
        if cut < width:
            copy.wait_recv()

            def far(rows, columns):
                inner = pl.ds(pl.multiple_of(columns.start - cut, 512), 512)
                total = inputs[rows, columns].astype(jnp.float32) + gathered(0, rows, columns)
                total = total + self.last[rows, inner].astype(jnp.float32)
                out[rows, columns] = total.astype(jnp.bfloat16)

            over_tiles(cut, width, far)
        for sent in self.sent:
            sent.wait_send()


def norm_into(inputs, gain, whole, rank):
    @pl.loop(0, BLOCK // 16)
    def _(r):
        values = inputs[pl.ds(pl.multiple_of(r * 16, 16), 16), :].astype(jnp.float32)
        mean = jnp.mean(values * values, axis=-1, keepdims=True)
        normed = (values * lax.rsqrt(mean + 1e-06) * gain[...]).astype(jnp.bfloat16)
        whole[pl.ds(pl.multiple_of(rank * BLOCK + r * 16, 16), 16), :] = normed


def hidden(tokens, gate_up, active, first_row, active_row):
    @pl.loop(0, gate_up.shape[2] // TILE)
    def _(n):
        columns = pl.ds(pl.multiple_of(n * TILE, TILE), TILE)
        rows_in = tokens[pl.ds(first_row, PLANE), :]
        gate = jnp.dot(rows_in, gate_up[0, :, columns], preferred_element_type=jnp.float32)
        up = jnp.dot(rows_in, gate_up[1, :, columns], preferred_element_type=jnp.float32)
        active[pl.ds(active_row, PLANE), columns] = (jax.nn.silu(gate) * up).astype(jnp.bfloat16)


def project(active, down, all_mix, partial, m, first_row, active_row, lane):
    mix = all_mix[pl.ds(first_row, PLANE), :]
    lanes = lax.broadcasted_iota(jnp.int32, mix.shape, 1)
    weight = jnp.sum(jnp.where(lanes == lane, mix, 0.0), axis=-1, keepdims=True)

    @pl.loop(0, down.shape[1] // TILE)
    def _(n):
        columns = pl.ds(pl.multiple_of(n * TILE, TILE), TILE)
        result = jnp.dot(
            active[pl.ds(active_row, PLANE), :], down[:, columns], preferred_element_type=jnp.float32
        )
        partial[m, :, columns] = (result * weight).astype(jnp.bfloat16)


def plane_row(rank, m):
    return pl.multiple_of(along_z(rank, HOMES[m]) // 4 * PLANE, PLANE)


def first_kernel(
    inputs, gain, mix, gate_up, down, first, second,
    full_gate_up, full_down, got_gate_up, got_down, got_first, got_second, mix_out, out,
    tokens, all_mix, w_gate_up, w_down, active, partial, theirs, over_x, from_z,
    y_send, y_recv, here, trade_send, trade_recv, d_send, d_recv, m_send, m_recv, c_send, c_recv,
):
    rank, place = lax.axis_index("expert"), lax.axis_index("dp")
    right, left = lax.rem(place + 1, 4), lax.rem(place + 3, 4)
    width = inputs.shape[1]
    greet([{"dp": right}, {"dp": left}] + group(rank))
    deep, low = gate_up.shape[1], down.shape[0]
    half = low // 2

    def gate_part(ref, k, owner):
        return ref.at[k, pl.ds(pl.multiple_of(owner * deep, deep), deep)]

    def down_part(ref, k, owner):
        return ref.at[pl.ds(pl.multiple_of(owner * low + k * half, half), half)]

    own = [gate_up.at[0], gate_up.at[1], down.at[pl.ds(0, half)], down.at[pl.ds(half, half)]]
    parts = [functools.partial(gate_part, full_gate_up, 0), functools.partial(gate_part, full_gate_up, 1),
             functools.partial(down_part, full_down, 0), functools.partial(down_part, full_down, 1)]
    nearby = [functools.partial(gate_part, w_gate_up, 0), functools.partial(gate_part, w_gate_up, 1),
              functools.partial(down_part, w_down, 0), functools.partial(down_part, w_down, 1)]

    def sems(k, i):
        return (y_send.at[k, i], y_recv.at[k, i])

    ways = [
        (remote(own[k], parts[k](place), sems(k, 0), {"dp": right}),
         remote(own[k], parts[k](place), sems(k, 1), {"dp": left}))
        for k in range(4)
    ]
    passes = [
        remote(parts[k](left), parts[k](left), sems(k, 2), {"dp": right}) if k % 2 == 0
        else remote(parts[k](right), parts[k](right), sems(k, 2), {"dp": left})
        for k in range(4)
    ]
    local = []

    def local_copy(src, dst, i):
        copy = pltpu.make_async_copy(src, dst, here.at[i])
        copy.start()
        local.append(copy)
        return copy

    def send_own(k):
        ways[k][0].start()
        ways[k + 1][1].start()
        ways[k + 1][0].start()
        ways[k][1].start()

    opposite = lax.rem(place + 2, 4)
    send_own(0)
    norm_into(inputs, gain, tokens, rank)
    spread = Spread(tokens, width, (d_send, d_recv), rank)
    spread.begin()
    all_mix[pl.ds(pl.multiple_of(rank * BLOCK, BLOCK), BLOCK), :] = mix[...]
    mixes = Spread(all_mix, all_mix.shape[1], (m_send, m_recv), rank)
    mixes.begin()
    for k in range(4):
        local_copy(own[k], parts[k](place), k)
        local_copy(own[k], nearby[k](place), 4 + k)

    spreads = (spread, mixes)
    for one in spreads:
        one.forward_x_arrival()
    for i in range(3):
        for one in spreads:
            one.forward_z_arrival(i)
    trades = []
    for i, (src, dst) in enumerate(
        ((gate_up, got_gate_up), (down, got_down), (first, got_first), (second, got_second))
    ):
        copy = remote(src, dst, (trade_send.at[i], trade_recv.at[i]), {"expert": rank ^ 8})
        copy.start()
        trades.append(copy)

    def pass_on(k):
        for j in (k, k + 1):
            ways[j][j % 2].wait_recv()
            passes[j].start()

    def land(k):
        for j in (k, k + 1):
            ways[j][1 - j % 2].wait_recv()
            local_copy(parts[j](left), nearby[j](left), 8 + j)
            local_copy(parts[j](right), nearby[j](right), 12 + j)

    def land_passed(k):
        for j in (k, k + 1):
            passes[j].wait_recv()
            local_copy(parts[j](opposite), nearby[j](opposite), 16 + j)

    pass_on(0)
    send_own(2)
    land(0)
    for i in range(3):
        for one in spreads:
            one.forward_far_arrival(i)
    for one in spreads:
        one.wait_own_plane()
        for i in range(3):
            one.wait_plane(i)
    land_passed(0)
    pass_on(2)
    land(2)
    for copy in local:
        copy.wait()
    local.clear()

    @pl.loop(0, 4)
    def _(b):
        row = pl.multiple_of(b * PLANE, PLANE)
        hidden(tokens, w_gate_up, active, row, row)

    land_passed(2)
    for copy in local:
        copy.wait()
    local.clear()
    keep = local_copy(all_mix, mix_out, 0)

    combine = Combine(partial, theirs, over_x, from_z, None, None, width, (c_send, c_recv), rank)
    order = (3, 1, 2, 0)
    for i, m in enumerate(order):
        row = plane_row(rank, m)
        project(active, w_down, all_mix, partial, m, row, row, rank)
        combine.to_sibling(m)
        if i:
            combine.add_sibling(order[i - 1])
        if i > 1:
            combine.add_x(order[i - 2])
    combine.add_sibling(order[3])
    combine.add_x(order[2])
    combine.add_x(order[3])
    combine.finish(inputs, out)
    keep.wait()
    for one in spreads:
        one.finish()
    for k in range(4):
        ways[k][0].wait_send()
        ways[k][1].wait_send()
        passes[k].wait_send()
    for copy in trades:
        copy.wait_recv()
    for copy in trades:
        copy.wait_send()


def bf16(*shape):
    return jax.ShapeDtypeStruct(shape, jnp.bfloat16)


def token_scratch(width, hidden_width, active_rows):
    return [
        pltpu.VMEM((2, width, hidden_width), jnp.bfloat16),
        pltpu.VMEM((hidden_width, width), jnp.bfloat16),
        pltpu.VMEM((active_rows, hidden_width), jnp.bfloat16),
        pltpu.VMEM((4, PLANE, width), jnp.bfloat16),
        pltpu.VMEM((4, 2, BLOCK, width), jnp.bfloat16),
        pltpu.VMEM((4, BLOCK, width), jnp.bfloat16),
        pltpu.VMEM((3, BLOCK, width), jnp.bfloat16),
    ]


def first_tick(inputs, gain, mix, gate_up, down, first, second):
    width, hidden_width = inputs.shape[1], gate_up.shape[2]
    rows = EXPERTS * BLOCK
    return pl.pallas_call(
        first_kernel,
        out_shape=(
            bf16(2, width, hidden_width), bf16(hidden_width, width),
            bf16(*gate_up.shape), bf16(*down.shape), bf16(*down.shape), bf16(*down.shape),
            jax.ShapeDtypeStruct((rows, 128), jnp.float32), bf16(*inputs.shape),
        ),
        in_specs=[VMEM] * 3 + [ANY] * 4,
        out_specs=[ANY] * 7 + [VMEM],
        scratch_shapes=[
            pltpu.VMEM((rows, width), jnp.bfloat16),
            pltpu.VMEM((rows, 128), jnp.float32),
            *token_scratch(width, hidden_width, rows),
            DMA((4, 3)), DMA((4, 3)), DMA((20,)), DMA((4,)), DMA((4,)),
            DMA((18,)), DMA((18,)), DMA((18,)), DMA((18,)), DMA((25,)), DMA((25,)),
        ],
        compiler_params=pltpu.CompilerParams(
            collective_id=0, has_side_effects=True, vmem_limit_bytes=60 << 20
        ),
        name="first_tick",
    )(inputs, gain, mix, gate_up, down, first, second)


def second_kernel(
    cut, inputs, gain, mix, full_gate_up, full_down, out,
    tokens, w_gate_up, w_down, active, partial, theirs, over_x, from_z, halves, last,
    here, d_send, d_recv, c_send, c_recv,
):
    rank = lax.axis_index("expert")
    greet(group(rank))
    loads = []
    for i, (src, dst) in enumerate(((full_gate_up, w_gate_up), (full_down, w_down))):
        copy = pltpu.make_async_copy(src, dst, here.at[i])
        copy.start()
        loads.append(copy)
    norm_into(inputs, gain, tokens, rank)
    spread = Spread(tokens, cut, (d_send, d_recv), rank)
    spread.begin()
    combine = Combine(partial, theirs, over_x, from_z, halves, last, cut, (c_send, c_recv), rank)

    def compute(m):
        row = plane_row(rank, m)
        hidden(tokens, w_gate_up, active, row, 0)
        project(active, w_down, mix, partial, m, row, 0, EXPERTS + rank)
        combine.to_sibling(m)

    spread.forward_x_arrival()
    for i in range(3):
        spread.forward_z_arrival(i)
    for copy in loads:
        copy.wait()
    spread.wait_own_plane()
    compute(0)
    spread.forward_far_arrival(0)
    spread.forward_far_arrival(1)
    combine.add_sibling(0)
    spread.wait_plane(0)
    compute(1)
    spread.forward_far_arrival(2)
    combine.add_x(0)
    combine.add_sibling(1)
    spread.wait_plane(1)
    compute(2)
    combine.add_x(1)
    combine.add_sibling(2)
    spread.wait_plane(2)
    compute(3)
    combine.add_x(2)
    combine.add_sibling(3)
    combine.add_x(3)
    combine.finish(inputs, out)
    spread.finish()


def second_tick(inputs, gain, mix, full_gate_up, full_down):
    width, hidden_width = inputs.shape[1], full_gate_up.shape[2]
    cut = 2560
    return pl.pallas_call(
        functools.partial(second_kernel, cut),
        out_shape=bf16(*inputs.shape),
        in_specs=[VMEM] * 3 + [ANY] * 2,
        out_specs=VMEM,
        scratch_shapes=[
            pltpu.VMEM((EXPERTS * BLOCK, width), jnp.bfloat16),
            *token_scratch(width, hidden_width, PLANE),
            pltpu.VMEM((3, 2, BLOCK, width - cut), jnp.bfloat16),
            pltpu.VMEM((BLOCK, width - cut), jnp.bfloat16),
            DMA((2,)), DMA((18,)), DMA((18,)), DMA((25,)), DMA((25,)),
        ],
        compiler_params=pltpu.CompilerParams(
            collective_id=1, has_side_effects=True, vmem_limit_bytes=60 << 20
        ),
        name="second_tick",
    )(inputs, gain, mix, full_gate_up, full_down)


def shifted(value, axis, distance):
    devices = range(lax.axis_size(axis))
    route = [(i - distance, i) for i in devices if i - distance in devices]
    return lax.ppermute(value, axis, route)


def per_device(
    fresh_tokens,
    in_flight,
    norm_weight,
    gate_up,
    down_proj,
    first_moment,
    second_moment,
    route_ids,
    route_probs,
    trade_flags,
):
    half_span = lax.axis_size("expert") // 2
    own_rank = lax.axis_index("expert")
    section_index = lax.axis_index("section")

    lanes = jnp.arange(128, dtype=jnp.int32)
    probs = route_probs[0]
    mix = probs / jnp.sum(probs, axis=-1, keepdims=True)
    wanted = route_ids[0] + EXPERTS * jnp.arange(2, dtype=jnp.int32)[:, None, None]
    dense_mix = jnp.sum(jnp.where(wanted[..., None] == lanes, mix[..., None], 0.0), axis=(0, 2))

    first_input = jnp.where(section_index == 0, fresh_tokens[0], in_flight)
    full_gate_up, full_down, *traded, all_mix, tick_zero = first_tick(
        first_input, norm_weight, dense_mix,
        gate_up[0, 0], down_proj[0, 0], first_moment[0, 0], second_moment[0, 0],
    )
    arrived = shifted(tick_zero, "section", 1)
    second_input = jnp.where(section_index == 0, fresh_tokens[1], arrived)
    tick_one = second_tick(second_input, norm_weight, all_mix, full_gate_up, full_down)
    layer_out = jnp.stack([tick_zero, tick_one])[None]

    moves = trade_flags[own_rank % half_span, 0] == 1
    kept = (gate_up, down_proj, first_moment, second_moment)
    moved = [
        jnp.where(moves, got.reshape(own.shape), own) for got, own in zip(traded, kept)
    ]
    return (layer_out, *moved)


def solution(mesh):
    return jax.shard_map(
        per_device,
        mesh=mesh,
        in_specs=(
            P(None, ("expert", "dp"), None),
            P(("expert", "dp"), None),
            P("section", None),
            P("section", "expert", None, "dp", None),
            P("section", "expert", "dp", None),
            P("section", "expert", "dp", None),
            P("section", "expert", "dp", None),
            P("section", None, ("expert", "dp"), None),
            P("section", None, ("expert", "dp"), None),
            P(),
        ),
        out_specs=(
            P("section", None, ("expert", "dp"), None),
            P("section", "expert", None, "dp", None),
            P("section", "expert", "dp", None),
            P("section", "expert", "dp", None),
            P("section", "expert", "dp", None),
        ),
        check_vma=False,
    )
```

```python
import functools

import jax
import jax.numpy as jnp
from jax import lax
from jax.experimental import pallas as pl
from jax.experimental.pallas import tpu as pltpu
from jax.sharding import PartitionSpec as P

EXPERTS = 16
BLOCK = 64
PLANE = 4 * BLOCK
HALF = BLOCK // 2
TILE = 256
MESH = pl.DeviceIdType.MESH
ANY = pl.BlockSpec(memory_space=pl.ANY)
VMEM = pl.BlockSpec(memory_space=pltpu.VMEM)
DMA = pltpu.SemaphoreType.DMA
STEPS = (1, 3, 2)
HOMES = (0, 3, 1, 2)


def along_z(rank, step):
    return lax.rem(rank + 4 * step, EXPERTS)


def remote(src, dst, sems, device):
    return pltpu.make_async_remote_copy(
        src_ref=src,
        dst_ref=dst,
        send_sem=sems[0],
        recv_sem=sems[1],
        device_id=device,
        device_id_type=MESH,
    )


def greet(devices):
    barrier = pltpu.get_barrier_semaphore()
    for device in devices:
        pl.semaphore_signal(barrier, inc=1, device_id=device, device_id_type=MESH)
    pl.semaphore_wait(barrier, len(devices))


def group(rank):
    return [{"expert": along_z(rank, step)} for step in STEPS] + [
        {"expert": rank ^ 2},
        {"expert": rank ^ 1},
    ]


def over_tiles(low, high, body):
    @pl.loop(0, BLOCK // 16)
    def _(r):
        rows = pl.ds(pl.multiple_of(r * 16, 16), 16)

        @pl.loop(low // 512, high // 512)
        def _(c):
            body(rows, pl.ds(pl.multiple_of(c * 512, 512), 512))


class Spread:
    def __init__(self, whole, cut, sems, rank, first_row=0, count=BLOCK):
        self.whole, self.cut, self.rank = whole, cut, rank
        self.first_row, self.count = first_row, count
        self.width = whole.shape[1]
        self.sems = sems
        self.sources = [along_z(rank, 4 - step) for step in STEPS]
        self.sent = []
        own = self.at(rank)
        self.first = [
            self.copy(own, i, {"expert": along_z(rank, step)}) for i, step in enumerate(STEPS)
        ]
        self.first.append(self.copy(own, 3, {"expert": rank ^ 2}))
        self.first.append(self.copy(own, 4, {"expert": rank ^ 1}))
        self.over_x, self.over_z, self.siblings = [], [], {}

    def at(self, owner, low=0, high=None):
        rows = pl.ds(pl.multiple_of(owner * BLOCK + self.first_row, self.count), self.count)
        if low == 0 and high is None:
            return self.whole.at[rows]
        return self.whole.at[rows, pl.ds(low, high - low)]

    def copy(self, ref, i, device):
        return remote(ref, ref, (self.sems[0].at[i], self.sems[1].at[i]), device)

    def start(self, copy):
        copy.start()
        self.sent.append(copy)
        return copy

    def begin(self):
        for copy in self.first:
            self.start(copy)

    def to_sibling(self, key, owner, i):
        self.siblings[key] = self.start(self.copy(self.at(owner), i, {"expert": self.rank ^ 1}))

    def forward_x_arrival(self):
        self.first[3].wait_recv()
        if self.cut < self.width:
            for i, step in enumerate(STEPS):
                ref = self.at(self.rank ^ 2, self.cut, self.width)
                self.over_z.append(
                    self.start(self.copy(ref, 8 + i, {"expert": along_z(self.rank, step)}))
                )
        self.to_sibling("x", self.rank ^ 2, 11)

    def forward_z_arrival(self, i):
        self.first[i].wait_recv()
        high = None if self.cut == self.width else self.cut
        self.over_x.append(
            self.start(self.copy(self.at(self.sources[i], 0, high), 5 + i, {"expert": self.rank ^ 2}))
        )
        self.to_sibling(("z", i), self.sources[i], 12 + i)

    def forward_far_arrival(self, i):
        self.over_x[i].wait_recv()
        if self.over_z:
            self.over_z[i].wait_recv()
        self.to_sibling(("far", i), self.sources[i] ^ 2, 15 + i)

    def wait_own_plane(self):
        self.first[4].wait_recv()
        self.siblings["x"].wait_recv()

    def wait_plane(self, i):
        self.siblings[("z", i)].wait_recv()
        self.siblings[("far", i)].wait_recv()

    def finish(self):
        for copy in self.sent:
            copy.wait_send()


class Combine:
    def __init__(self, partial, theirs, over_x, from_z, halves, last, cut, sems, rank):
        self.partial, self.theirs, self.over_x, self.from_z = partial, theirs, over_x, from_z
        self.halves, self.last, self.cut, self.rank = halves, last, cut, rank
        self.width = partial.shape[2]
        self.send, self.recv = sems
        self.side = lax.rem(rank // 2, 2)
        self.core = lax.rem(rank, 2)
        self.sent = []
        self.sibling, self.x_copies, self.z_copies, self.half_copies = {}, {}, {}, {}

    def start(self, src, dst, i, device):
        copy = remote(src, dst, (self.send.at[i], self.recv.at[i]), {"expert": device})
        copy.start()
        self.sent.append(copy)
        return copy

    def rows(self, dx, core):
        side = self.side if dx == 0 else 1 - self.side
        return pl.multiple_of((side * 2 + core) * BLOCK, BLOCK)

    def to_sibling(self, m):
        for dx in (1, 0):
            src = self.partial.at[m, pl.ds(self.rows(dx, 1 - self.core), BLOCK)]
            self.sibling[m, dx] = self.start(src, self.theirs.at[m, dx], 2 * m + dx, self.rank ^ 1)

    def add_sibling(self, m):
        peer = along_z(self.rank, HOMES[m])
        for dx in (1, 0):
            self.sibling[m, dx].wait_recv()
            base = self.rows(dx, self.core)

            def body(rows, columns):
                mine = self.partial[m, pl.ds(pl.multiple_of(base + rows.start, 16), 16), columns]
                total = mine.astype(jnp.float32) + self.theirs[m, dx, rows, columns].astype(jnp.float32)
                self.theirs[m, dx, rows, columns] = total.astype(jnp.bfloat16)

            over_tiles(0, self.width, body)
            if dx == 1:
                below = pl.ds(0, self.cut)
                self.x_copies[m] = self.start(
                    self.theirs.at[m, 1, :, below], self.over_x.at[m, :, below], 8 + m, self.rank ^ 2
                )
            if self.cut < self.width and m:
                above = pl.ds(self.cut, self.width - self.cut)
                self.half_copies[m, dx] = self.start(
                    self.theirs.at[m, dx, :, above], self.halves.at[m - 1, dx], 12 + 2 * m + dx, peer
                )

    def add_x(self, m):
        self.x_copies[m].wait_recv()

        def body(rows, columns):
            total = self.over_x[m, rows, columns].astype(jnp.float32)
            total = total + self.theirs[m, 0, rows, columns].astype(jnp.float32)
            self.over_x[m, rows, columns] = total.astype(jnp.bfloat16)

        over_tiles(0, self.cut, body)
        if m:
            below = pl.ds(0, self.cut)
            self.z_copies[m] = self.start(
                self.over_x.at[m, :, below], self.from_z.at[m - 1, :, below], 20 + m,
                along_z(self.rank, HOMES[m]),
            )

    def finish(self, inputs, out):
        cut, width = self.cut, self.width
        if cut < width:
            for m in (1, 2, 3):
                for dx in (1, 0):
                    self.half_copies[m, dx].wait_recv()

            def gathered(dx, rows, columns):
                total = self.theirs[0, dx, rows, columns].astype(jnp.float32)
                inner = pl.ds(pl.multiple_of(columns.start - cut, 512), 512)
                for m in range(3):
                    total = total + self.halves[m, dx, rows, inner].astype(jnp.float32)
                return total

            def other(rows, columns):
                self.theirs[0, 1, rows, columns] = gathered(1, rows, columns).astype(jnp.bfloat16)

            over_tiles(cut, width, other)
            above = pl.ds(cut, width - cut)
            copy = self.start(self.theirs.at[0, 1, :, above], self.last, 24, self.rank ^ 2)

        for m in (1, 2, 3):
            self.z_copies[m].wait_recv()

        def near(rows, columns):
            total = inputs[rows, columns].astype(jnp.float32)
            total = total + self.over_x[0, rows, columns].astype(jnp.float32)
            for m in range(3):
                total = total + self.from_z[m, rows, columns].astype(jnp.float32)
            out[rows, columns] = total.astype(jnp.bfloat16)

        over_tiles(0, cut, near)
        if cut < width:
            copy.wait_recv()

            def far(rows, columns):
                inner = pl.ds(pl.multiple_of(columns.start - cut, 512), 512)
                total = inputs[rows, columns].astype(jnp.float32) + gathered(0, rows, columns)
                total = total + self.last[rows, inner].astype(jnp.float32)
                out[rows, columns] = total.astype(jnp.bfloat16)

            over_tiles(cut, width, far)
        for sent in self.sent:
            sent.wait_send()


def norm_into(inputs, gain, whole, rank, first_row=0, count=BLOCK):
    @pl.loop(first_row // 16, (first_row + count) // 16)
    def _(r):
        values = inputs[pl.ds(pl.multiple_of(r * 16, 16), 16), :].astype(jnp.float32)
        mean = jnp.mean(values * values, axis=-1, keepdims=True)
        normed = (values * lax.rsqrt(mean + 1e-06) * gain[...]).astype(jnp.bfloat16)
        whole[pl.ds(pl.multiple_of(rank * BLOCK + r * 16, 16), 16), :] = normed


def hidden(tokens, gate_up, active, first_row, active_row):
    rows_in = tokens[pl.ds(first_row, PLANE), :]
    gate = jnp.dot(rows_in, gate_up[0], preferred_element_type=jnp.float32)
    up = jnp.dot(rows_in, gate_up[1], preferred_element_type=jnp.float32)
    active[pl.ds(active_row, PLANE), :] = (jax.nn.silu(gate) * up).astype(jnp.bfloat16)


def project(active, down, all_mix, partial, m, first_row, active_row, lane):
    mix = all_mix[pl.ds(first_row, PLANE), :]
    lanes = lax.broadcasted_iota(jnp.int32, mix.shape, 1)
    weight = jnp.sum(jnp.where(lanes == lane, mix, 0.0), axis=-1, keepdims=True)

    @pl.loop(0, down.shape[1] // TILE, unroll=True)
    def _(n):
        columns = pl.ds(pl.multiple_of(n * TILE, TILE), TILE)
        result = jnp.dot(
            active[pl.ds(active_row, PLANE), :], down[:, columns], preferred_element_type=jnp.float32
        )
        partial[m, :, columns] = (result * weight).astype(jnp.bfloat16)


def plane_row(rank, m):
    return pl.multiple_of(along_z(rank, HOMES[m]) // 4 * PLANE, PLANE)


def first_kernel(
    inputs, gain, mix, gate_up, down, first, second,
    full_gate_up, full_down, got_gate_up, got_down, got_first, got_second, mix_out, out,
    tokens, all_mix, w_gate_up, w_down, active, partial, theirs, over_x, from_z,
    y_send, y_recv, here, trade_send, trade_recv, d_send, d_recv, m_send, m_recv, c_send, c_recv,
):
    rank, place = lax.axis_index("expert"), lax.axis_index("dp")
    right, left = lax.rem(place + 1, 4), lax.rem(place + 3, 4)
    width = inputs.shape[1]
    greet([{"dp": right}, {"dp": left}] + group(rank))
    deep, low = gate_up.shape[1], down.shape[0]
    half = low // 2

    def gate_part(ref, k, owner):
        return ref.at[k, pl.ds(pl.multiple_of(owner * deep, deep), deep)]

    def down_part(ref, k, owner):
        return ref.at[pl.ds(pl.multiple_of(owner * low + k * half, half), half)]

    own = [gate_up.at[0], gate_up.at[1], down.at[pl.ds(0, half)], down.at[pl.ds(half, half)]]
    parts = [functools.partial(gate_part, w_gate_up, 0), functools.partial(gate_part, w_gate_up, 1),
             functools.partial(down_part, w_down, 0), functools.partial(down_part, w_down, 1)]

    def sems(k, i):
        return (y_send.at[k, i], y_recv.at[k, i])

    ways = [
        (remote(own[k], parts[k](place), sems(k, 0), {"dp": right}),
         remote(own[k], parts[k](place), sems(k, 1), {"dp": left}))
        for k in range(4)
    ]
    passes = [
        remote(parts[k](left), parts[k](left), sems(k, 2), {"dp": right}) if k % 2 == 0
        else remote(parts[k](right), parts[k](right), sems(k, 2), {"dp": left})
        for k in range(4)
    ]
    local = []

    def local_copy(src, dst, i):
        copy = pltpu.make_async_copy(src, dst, here.at[i])
        copy.start()
        local.append(copy)
        return copy

    def send_own(k):
        ways[k][0].start()
        ways[k + 1][1].start()
        ways[k + 1][0].start()
        ways[k][1].start()

    for k in range(4):
        local_copy(own[k], parts[k](place), k)
    send_own(0)
    norm_into(inputs, gain, tokens, rank)
    spread = Spread(tokens, width, (d_send, d_recv), rank)
    spread.begin()
    all_mix[pl.ds(pl.multiple_of(rank * BLOCK, BLOCK), BLOCK), :] = mix[...]
    mixes = Spread(all_mix, all_mix.shape[1], (m_send, m_recv), rank)
    mixes.begin()
    spreads = (spread, mixes)
    for one in spreads:
        one.forward_x_arrival()
    for i in range(3):
        for one in spreads:
            one.forward_z_arrival(i)
    trades = []
    for i, (src, dst) in enumerate(
        ((gate_up, got_gate_up), (down, got_down), (first, got_first), (second, got_second))
    ):
        copy = remote(src, dst, (trade_send.at[i], trade_recv.at[i]), {"expert": rank ^ 8})
        copy.start()
        trades.append(copy)

    def pass_on(k):
        for j in (k, k + 1):
            ways[j][j % 2].wait_recv()
            passes[j].start()

    def land(k):
        for j in (k, k + 1):
            ways[j][1 - j % 2].wait_recv()

    def land_passed(k):
        for j in (k, k + 1):
            passes[j].wait_recv()

    pass_on(0)
    land(0)
    for i in range(3):
        for one in spreads:
            one.forward_far_arrival(i)
    for one in spreads:
        one.wait_own_plane()
        for i in range(3):
            one.wait_plane(i)
    land_passed(0)
    send_own(2)
    for copy in local:
        copy.wait()
    local.clear()

    @pl.loop(0, 4)
    def _(b):
        row = pl.multiple_of(b * PLANE, PLANE)
        hidden(tokens, w_gate_up, active, row, row)

    pass_on(2)
    land(2)
    land_passed(2)
    kept = [
        local_copy(w_gate_up, full_gate_up, 0),
        local_copy(w_down, full_down, 1),
        local_copy(all_mix, mix_out, 2),
    ]

    combine = Combine(partial, theirs, over_x, from_z, None, None, width, (c_send, c_recv), rank)
    order = (3, 1, 2, 0)
    for i, m in enumerate(order):
        row = plane_row(rank, m)
        project(active, w_down, all_mix, partial, m, row, row, rank)
        combine.to_sibling(m)
        if i:
            combine.add_sibling(order[i - 1])
        if i > 1:
            combine.add_x(order[i - 2])
    combine.add_sibling(order[3])
    combine.add_x(order[2])
    combine.add_x(order[3])
    combine.finish(inputs, out)
    for copy in kept:
        copy.wait()
    for one in spreads:
        one.finish()
    for k in range(4):
        ways[k][0].wait_send()
        ways[k][1].wait_send()
        passes[k].wait_send()
    for copy in trades:
        copy.wait_recv()
    for copy in trades:
        copy.wait_send()


def bf16(*shape):
    return jax.ShapeDtypeStruct(shape, jnp.bfloat16)


def token_scratch(width, hidden_width, active_rows):
    return [
        pltpu.VMEM((2, width, hidden_width), jnp.bfloat16),
        pltpu.VMEM((hidden_width, width), jnp.bfloat16),
        pltpu.VMEM((active_rows, hidden_width), jnp.bfloat16),
        pltpu.VMEM((4, PLANE, width), jnp.bfloat16),
        pltpu.VMEM((4, 2, BLOCK, width), jnp.bfloat16),
        pltpu.VMEM((4, BLOCK, width), jnp.bfloat16),
        pltpu.VMEM((3, BLOCK, width), jnp.bfloat16),
    ]


def first_tick(inputs, gain, mix, gate_up, down, first, second):
    width, hidden_width = inputs.shape[1], gate_up.shape[2]
    rows = EXPERTS * BLOCK
    return pl.pallas_call(
        first_kernel,
        out_shape=(
            bf16(2, width, hidden_width), bf16(hidden_width, width),
            bf16(*gate_up.shape), bf16(*down.shape), bf16(*down.shape), bf16(*down.shape),
            jax.ShapeDtypeStruct((rows, 128), jnp.float32), bf16(*inputs.shape),
        ),
        in_specs=[VMEM] * 3 + [ANY] * 4,
        out_specs=[ANY] * 7 + [VMEM],
        scratch_shapes=[
            pltpu.VMEM((rows, width), jnp.bfloat16),
            pltpu.VMEM((rows, 128), jnp.float32),
            *token_scratch(width, hidden_width, rows),
            DMA((4, 3)), DMA((4, 3)), DMA((4,)), DMA((4,)), DMA((4,)),
            DMA((18,)), DMA((18,)), DMA((18,)), DMA((18,)), DMA((25,)), DMA((25,)),
        ],
        compiler_params=pltpu.CompilerParams(
            collective_id=0, has_side_effects=True, vmem_limit_bytes=60 << 20
        ),
        name="first_tick",
    )(inputs, gain, mix, gate_up, down, first, second)


def second_kernel(
    cut, inputs, gain, mix, full_gate_up, full_down, out,
    tokens, w_gate_up, w_down, active, partial, theirs, over_x, from_z, halves, last,
    here, d_send, d_recv, c_send, c_recv,
):
    rank = lax.axis_index("expert")
    greet(group(rank))
    loads = []
    for i, (src, dst) in enumerate(((full_gate_up, w_gate_up), (full_down, w_down))):
        copy = pltpu.make_async_copy(src, dst, here.at[i])
        copy.start()
        loads.append(copy)
    spreads = []
    for i in range(2):
        norm_into(inputs, gain, tokens, rank, i * HALF, HALF)
        one = Spread(tokens, cut, (d_send.at[i], d_recv.at[i]), rank, i * HALF, HALF)
        one.begin()
        spreads.append(one)
    combine = Combine(partial, theirs, over_x, from_z, halves, last, cut, (c_send, c_recv), rank)

    def up(m):
        hidden(tokens, w_gate_up, active, plane_row(rank, m), 0)

    def project_out(m):
        project(active, w_down, mix, partial, m, plane_row(rank, m), 0, EXPERTS + rank)
        combine.to_sibling(m)

    def far(i):
        for one in spreads:
            one.forward_far_arrival(i)

    def wait_plane(i):
        for one in spreads:
            one.wait_plane(i)

    for one in spreads:
        one.forward_x_arrival()
        for i in range(3):
            one.forward_z_arrival(i)
    for copy in loads:
        copy.wait()
    for one in spreads:
        one.wait_own_plane()
    up(0)
    far(0)
    project_out(0)
    far(1)
    wait_plane(0)
    up(1)
    far(2)
    combine.add_sibling(0)
    project_out(1)
    wait_plane(1)
    up(2)
    combine.add_sibling(1)
    project_out(2)
    combine.add_x(0)
    wait_plane(2)
    up(3)
    combine.add_sibling(2)
    project_out(3)
    combine.add_x(1)
    combine.add_sibling(3)
    combine.add_x(2)
    combine.add_x(3)
    combine.finish(inputs, out)
    for one in spreads:
        one.finish()


def second_tick(inputs, gain, mix, full_gate_up, full_down):
    width, hidden_width = inputs.shape[1], full_gate_up.shape[2]
    cut = 2560
    return pl.pallas_call(
        functools.partial(second_kernel, cut),
        out_shape=bf16(*inputs.shape),
        in_specs=[VMEM] * 3 + [ANY] * 2,
        out_specs=VMEM,
        scratch_shapes=[
            pltpu.VMEM((EXPERTS * BLOCK, width), jnp.bfloat16),
            *token_scratch(width, hidden_width, PLANE),
            pltpu.VMEM((3, 2, BLOCK, width - cut), jnp.bfloat16),
            pltpu.VMEM((BLOCK, width - cut), jnp.bfloat16),
            DMA((2,)), DMA((2, 18)), DMA((2, 18)), DMA((25,)), DMA((25,)),
        ],
        compiler_params=pltpu.CompilerParams(
            collective_id=1, has_side_effects=True, vmem_limit_bytes=60 << 20
        ),
        name="second_tick",
    )(inputs, gain, mix, full_gate_up, full_down)


def shifted(value, axis, distance):
    devices = range(lax.axis_size(axis))
    route = [(i - distance, i) for i in devices if i - distance in devices]
    return lax.ppermute(value, axis, route)


def per_device(
    fresh_tokens,
    in_flight,
    norm_weight,
    gate_up,
    down_proj,
    first_moment,
    second_moment,
    route_ids,
    route_probs,
    trade_flags,
):
    half_span = lax.axis_size("expert") // 2
    own_rank = lax.axis_index("expert")
    section_index = lax.axis_index("section")

    lanes = jnp.arange(128, dtype=jnp.int32)
    probs = route_probs[0]
    mix = probs / jnp.sum(probs, axis=-1, keepdims=True)
    wanted = route_ids[0] + EXPERTS * jnp.arange(2, dtype=jnp.int32)[:, None, None]
    dense_mix = jnp.sum(jnp.where(wanted[..., None] == lanes, mix[..., None], 0.0), axis=(0, 2))

    first_input = jnp.where(section_index == 0, fresh_tokens[0], in_flight)
    full_gate_up, full_down, *traded, all_mix, tick_zero = first_tick(
        first_input, norm_weight, dense_mix,
        gate_up[0, 0], down_proj[0, 0], first_moment[0, 0], second_moment[0, 0],
    )
    arrived = shifted(tick_zero, "section", 1)
    second_input = jnp.where(section_index == 0, fresh_tokens[1], arrived)
    tick_one = second_tick(second_input, norm_weight, all_mix, full_gate_up, full_down)
    layer_out = jnp.stack([tick_zero, tick_one])[None]

    moves = trade_flags[own_rank % half_span, 0] == 1
    kept = (gate_up, down_proj, first_moment, second_moment)
    moved = [
        jnp.where(moves, got.reshape(own.shape), own) for got, own in zip(traded, kept)
    ]
    return (layer_out, *moved)


def solution(mesh):
    return jax.shard_map(
        per_device,
        mesh=mesh,
        in_specs=(
            P(None, ("expert", "dp"), None),
            P(("expert", "dp"), None),
            P("section", None),
            P("section", "expert", None, "dp", None),
            P("section", "expert", "dp", None),
            P("section", "expert", "dp", None),
            P("section", "expert", "dp", None),
            P("section", None, ("expert", "dp"), None),
            P("section", None, ("expert", "dp"), None),
            P(),
        ),
        out_specs=(
            P("section", None, ("expert", "dp"), None),
            P("section", "expert", None, "dp", None),
            P("section", "expert", "dp", None),
            P("section", "expert", "dp", None),
            P("section", "expert", "dp", None),
        ),
        check_vma=False,
    )
```

```python
import functools

import jax
import jax.numpy as jnp
from jax import lax
from jax.experimental import pallas as pl
from jax.experimental.pallas import tpu as pltpu
from jax.sharding import PartitionSpec as P

EXPERTS = 16
BLOCK = 64
PLANE = 4 * BLOCK
HALF = BLOCK // 2
TILE = 1024
CHUNKS = 4
MESH = pl.DeviceIdType.MESH
ANY = pl.BlockSpec(memory_space=pl.ANY)
VMEM = pl.BlockSpec(memory_space=pltpu.VMEM)
DMA = pltpu.SemaphoreType.DMA
STEPS = (1, 3, 2)
HOMES = (0, 3, 1, 2)


def along_z(rank, step):
    return lax.rem(rank + 4 * step, EXPERTS)


def remote(src, dst, sems, device):
    return pltpu.make_async_remote_copy(
        src_ref=src,
        dst_ref=dst,
        send_sem=sems[0],
        recv_sem=sems[1],
        device_id=device,
        device_id_type=MESH,
    )


def greet(devices):
    barrier = pltpu.get_barrier_semaphore()
    for device in devices:
        pl.semaphore_signal(barrier, inc=1, device_id=device, device_id_type=MESH)
    pl.semaphore_wait(barrier, len(devices))


def group(rank):
    return [{"expert": along_z(rank, step)} for step in STEPS] + [
        {"expert": rank ^ 2},
        {"expert": rank ^ 1},
    ]


def over_tiles(low, high, body):
    @pl.loop(0, BLOCK // 16)
    def _(r):
        rows = pl.ds(pl.multiple_of(r * 16, 16), 16)

        @pl.loop(low // 512, high // 512)
        def _(c):
            body(rows, pl.ds(pl.multiple_of(c * 512, 512), 512))


class Spread:
    def __init__(self, whole, cut, sems, rank, first_row=0, count=BLOCK):
        self.whole, self.cut, self.rank = whole, cut, rank
        self.first_row, self.count = first_row, count
        self.width = whole.shape[1]
        self.sems = sems
        self.sources = [along_z(rank, 4 - step) for step in STEPS]
        self.sent = []
        own = self.at(rank)
        self.first = [
            self.copy(own, i, {"expert": along_z(rank, step)}) for i, step in enumerate(STEPS)
        ]
        self.first.append(self.copy(own, 3, {"expert": rank ^ 2}))
        self.first.append(self.copy(own, 4, {"expert": rank ^ 1}))
        self.over_x, self.over_z, self.siblings = [], [], {}

    def at(self, owner, low=0, high=None):
        rows = pl.ds(pl.multiple_of(owner * BLOCK + self.first_row, self.count), self.count)
        if low == 0 and high is None:
            return self.whole.at[rows]
        return self.whole.at[rows, pl.ds(low, high - low)]

    def copy(self, ref, i, device):
        return remote(ref, ref, (self.sems[0].at[i], self.sems[1].at[i]), device)

    def start(self, copy):
        copy.start()
        self.sent.append(copy)
        return copy

    def begin(self):
        for copy in self.first:
            self.start(copy)

    def to_sibling(self, key, owner, i):
        self.siblings[key] = self.start(self.copy(self.at(owner), i, {"expert": self.rank ^ 1}))

    def forward_x_arrival(self):
        self.first[3].wait_recv()
        if self.cut < self.width:
            for i, step in enumerate(STEPS):
                ref = self.at(self.rank ^ 2, self.cut, self.width)
                self.over_z.append(
                    self.start(self.copy(ref, 8 + i, {"expert": along_z(self.rank, step)}))
                )
        self.to_sibling("x", self.rank ^ 2, 11)

    def forward_z_arrival(self, i):
        self.first[i].wait_recv()
        high = None if self.cut == self.width else self.cut
        self.over_x.append(
            self.start(self.copy(self.at(self.sources[i], 0, high), 5 + i, {"expert": self.rank ^ 2}))
        )
        self.to_sibling(("z", i), self.sources[i], 12 + i)

    def forward_far_arrival(self, i):
        self.over_x[i].wait_recv()
        if self.over_z:
            self.over_z[i].wait_recv()
        self.to_sibling(("far", i), self.sources[i] ^ 2, 15 + i)

    def wait_own_plane(self):
        self.first[4].wait_recv()
        self.siblings["x"].wait_recv()

    def wait_plane(self, i):
        self.siblings[("z", i)].wait_recv()
        self.siblings[("far", i)].wait_recv()

    def finish(self):
        for copy in self.sent:
            copy.wait_send()


class Combine:
    def __init__(self, partial, theirs, over_x, from_z, halves, last, columns, sems, rank):
        self.partial, self.theirs, self.over_x, self.from_z = partial, theirs, over_x, from_z
        self.halves, self.last, self.rank = halves, last, rank
        self.low, self.cut, self.width = columns
        self.send, self.recv = sems
        self.side = lax.rem(rank // 2, 2)
        self.core = lax.rem(rank, 2)
        self.sent = []
        self.sibling, self.x_copies, self.z_copies, self.half_copies = {}, {}, {}, {}

    def start(self, src, dst, i, device):
        copy = remote(src, dst, (self.send.at[i], self.recv.at[i]), {"expert": device})
        copy.start()
        self.sent.append(copy)
        return copy

    def rows(self, dx, core):
        side = self.side if dx == 0 else 1 - self.side
        return pl.multiple_of((side * 2 + core) * BLOCK, BLOCK)

    def to_sibling(self, m):
        columns = pl.ds(self.low, self.width - self.low)
        for dx in (1, 0):
            src = self.partial.at[m, pl.ds(self.rows(dx, 1 - self.core), BLOCK), columns]
            self.sibling[m, dx] = self.start(
                src, self.theirs.at[m, dx, :, columns], 2 * m + dx, self.rank ^ 1
            )

    def add_sibling(self, m):
        peer = along_z(self.rank, HOMES[m])
        for dx in (1, 0):
            self.sibling[m, dx].wait_recv()
            base = self.rows(dx, self.core)

            def body(rows, columns):
                mine = self.partial[m, pl.ds(pl.multiple_of(base + rows.start, 16), 16), columns]
                total = mine.astype(jnp.float32) + self.theirs[m, dx, rows, columns].astype(jnp.float32)
                self.theirs[m, dx, rows, columns] = total.astype(jnp.bfloat16)

            over_tiles(self.low, self.width, body)
            if dx == 1:
                below = pl.ds(self.low, self.cut - self.low)
                self.x_copies[m] = self.start(
                    self.theirs.at[m, 1, :, below], self.over_x.at[m, :, below], 8 + m, self.rank ^ 2
                )
            if self.cut < self.width and m:
                above = pl.ds(self.cut, self.width - self.cut)
                self.half_copies[m, dx] = self.start(
                    self.theirs.at[m, dx, :, above], self.halves.at[m - 1, dx], 12 + 2 * m + dx, peer
                )

    def add_x(self, m):
        self.x_copies[m].wait_recv()

        def body(rows, columns):
            total = self.over_x[m, rows, columns].astype(jnp.float32)
            total = total + self.theirs[m, 0, rows, columns].astype(jnp.float32)
            self.over_x[m, rows, columns] = total.astype(jnp.bfloat16)

        over_tiles(self.low, self.cut, body)
        if m:
            below = pl.ds(self.low, self.cut - self.low)
            self.z_copies[m] = self.start(
                self.over_x.at[m, :, below], self.from_z.at[m - 1, :, below], 20 + m,
                along_z(self.rank, HOMES[m]),
            )

    def finish(self, inputs, out):
        cut, width = self.cut, self.width
        if cut < width:
            for m in (1, 2, 3):
                for dx in (1, 0):
                    self.half_copies[m, dx].wait_recv()

            def gathered(dx, rows, columns):
                total = self.theirs[0, dx, rows, columns].astype(jnp.float32)
                inner = pl.ds(pl.multiple_of(columns.start - cut, 512), 512)
                for m in range(3):
                    total = total + self.halves[m, dx, rows, inner].astype(jnp.float32)
                return total

            def other(rows, columns):
                self.theirs[0, 1, rows, columns] = gathered(1, rows, columns).astype(jnp.bfloat16)

            over_tiles(cut, width, other)
            above = pl.ds(cut, width - cut)
            copy = self.start(self.theirs.at[0, 1, :, above], self.last, 24, self.rank ^ 2)

        for m in (1, 2, 3):
            self.z_copies[m].wait_recv()

        def near(rows, columns):
            total = inputs[rows, columns].astype(jnp.float32)
            total = total + self.over_x[0, rows, columns].astype(jnp.float32)
            for m in range(3):
                total = total + self.from_z[m, rows, columns].astype(jnp.float32)
            out[rows, columns] = total.astype(jnp.bfloat16)

        over_tiles(self.low, cut, near)
        if cut < width:
            copy.wait_recv()

            def far(rows, columns):
                inner = pl.ds(pl.multiple_of(columns.start - cut, 512), 512)
                total = inputs[rows, columns].astype(jnp.float32) + gathered(0, rows, columns)
                total = total + self.last[rows, inner].astype(jnp.float32)
                out[rows, columns] = total.astype(jnp.bfloat16)

            over_tiles(cut, width, far)

    def drain(self):
        for sent in self.sent:
            sent.wait_send()


def norm_into(inputs, gain, whole, rank, first_row=0, count=BLOCK):
    @pl.loop(first_row // 16, (first_row + count) // 16)
    def _(r):
        values = inputs[pl.ds(pl.multiple_of(r * 16, 16), 16), :].astype(jnp.float32)
        mean = jnp.mean(values * values, axis=-1, keepdims=True)
        normed = (values * lax.rsqrt(mean + 1e-06) * gain[...]).astype(jnp.bfloat16)
        whole[pl.ds(pl.multiple_of(rank * BLOCK + r * 16, 16), 16), :] = normed


def hidden(tokens, gate_up, active, first_row, active_row):
    rows_in = tokens[pl.ds(first_row, PLANE), :]
    gate = jnp.dot(rows_in, gate_up[0], preferred_element_type=jnp.float32)
    up = jnp.dot(rows_in, gate_up[1], preferred_element_type=jnp.float32)
    active[pl.ds(active_row, PLANE), :] = (jax.nn.silu(gate) * up).astype(jnp.bfloat16)


def project(active, down, all_mix, partial, m, first_row, active_row, lane, low, high):
    mix = all_mix[pl.ds(first_row, PLANE), :]
    lanes = lax.broadcasted_iota(jnp.int32, mix.shape, 1)
    weight = jnp.sum(jnp.where(lanes == lane, mix, 0.0), axis=-1, keepdims=True)

    for start in range(low, high, TILE):
        columns = pl.ds(start, TILE)
        result = jnp.dot(
            active[pl.ds(active_row, PLANE), :], down[:, columns], preferred_element_type=jnp.float32
        )
        partial[m, :, columns] = (result * weight).astype(jnp.bfloat16)


def plane_row(rank, m):
    return pl.multiple_of(along_z(rank, HOMES[m]) // 4 * PLANE, PLANE)


def early(ref):
    return ref.at[pl.ds(0, ref.shape[0] // 3)]


def late(ref):
    middle = ref.shape[0] // 3
    return ref.at[pl.ds(middle, ref.shape[0] - middle)]


def first_kernel(
    inputs, gain, mix, gate_up, down, first, second,
    full_gate_up, full_down, got_gate_up, got_down, got_first, got_second, mix_out, out,
    tokens, all_mix, w_gate_up, w_down, active, partial, theirs, over_x, from_z,
    y_send, y_recv, here, trade_send, trade_recv, d_send, d_recv, m_send, m_recv, c_send, c_recv,
):
    rank, place = lax.axis_index("expert"), lax.axis_index("dp")
    right, left = lax.rem(place + 1, 4), lax.rem(place + 3, 4)
    width = inputs.shape[1]
    greet([{"dp": right}, {"dp": left}] + group(rank))
    deep, low = gate_up.shape[1], down.shape[0]
    half = low // 2

    def gate_part(ref, k, owner):
        return ref.at[k, pl.ds(pl.multiple_of(owner * deep, deep), deep)]

    chunk = width // CHUNKS

    def down_part(ref, k, owner):
        row, column = owner * low + k % 2 * half, k // 2 * chunk
        return ref.at[pl.ds(pl.multiple_of(row, half), half), pl.ds(column, chunk)]

    count = 2 + 2 * CHUNKS
    own = [gate_up.at[0], gate_up.at[1]] + [down_part(down, k, 0) for k in range(2 * CHUNKS)]
    parts = [functools.partial(gate_part, w_gate_up, 0), functools.partial(gate_part, w_gate_up, 1)]
    parts += [functools.partial(down_part, w_down, k) for k in range(2 * CHUNKS)]

    def sems(k, i):
        return (y_send.at[k, i], y_recv.at[k, i])

    ways = [
        (remote(own[k], parts[k](place), sems(k, 0), {"dp": right}),
         remote(own[k], parts[k](place), sems(k, 1), {"dp": left}))
        for k in range(count)
    ]
    passes = [
        remote(parts[k](left), parts[k](left), sems(k, 2), {"dp": right}) if k % 2 == 0
        else remote(parts[k](right), parts[k](right), sems(k, 2), {"dp": left})
        for k in range(count)
    ]
    local = []

    def local_copy(src, dst, i):
        copy = pltpu.make_async_copy(src, dst, here.at[i])
        copy.start()
        local.append(copy)
        return copy

    def send_own(k):
        ways[k][0].start()
        ways[k + 1][1].start()
        ways[k + 1][0].start()
        ways[k][1].start()

    for k in range(count):
        local_copy(own[k], parts[k](place), k)
    send_own(0)
    norm_into(inputs, gain, tokens, rank)
    spread = Spread(tokens, width, (d_send, d_recv), rank)
    spread.begin()
    all_mix[pl.ds(pl.multiple_of(rank * BLOCK, BLOCK), BLOCK), :] = mix[...]
    mixes = Spread(all_mix, all_mix.shape[1], (m_send, m_recv), rank)
    mixes.begin()
    spreads = (spread, mixes)
    for one in spreads:
        one.forward_x_arrival()
    for i in range(3):
        for one in spreads:
            one.forward_z_arrival(i)
    trades = []
    for i, (src, dst) in enumerate(
        ((gate_up, got_gate_up), (down, got_down), (first, got_first), (early(second), early(got_second)))
    ):
        copy = remote(src, dst, (trade_send.at[i], trade_recv.at[i]), {"expert": rank ^ 8})
        copy.start()
        trades.append(copy)

    def pass_on(k):
        for j in (k, k + 1):
            ways[j][j % 2].wait_recv()
            passes[j].start()

    def land(k):
        for j in (k, k + 1):
            ways[j][1 - j % 2].wait_recv()

    def land_passed(k):
        for j in (k, k + 1):
            passes[j].wait_recv()

    pass_on(0)
    land(0)
    for i in range(3):
        for one in spreads:
            one.forward_far_arrival(i)
    for one in spreads:
        one.wait_own_plane()
        for i in range(3):
            one.wait_plane(i)
    land_passed(0)
    send_own(2)
    send_own(4)
    for copy in local:
        copy.wait()
    local.clear()

    kept = []

    def keep(src, dst, i):
        kept.append(pltpu.make_async_copy(src, dst, here.at[i]))
        kept[-1].start()

    @pl.loop(0, 4)
    def _(b):
        row = pl.multiple_of(b * PLANE, PLANE)
        hidden(tokens, w_gate_up, active, row, row)

    combines = [
        Combine(
            partial, theirs, over_x, from_z, None, None, (c * chunk, (c + 1) * chunk, (c + 1) * chunk),
            (c_send.at[c], c_recv.at[c]), rank,
        )
        for c in range(CHUNKS)
    ]
    order = (3, 1, 2, 0)
    for c in range(CHUNKS):
        pass_on(2 + 2 * c)
        if c + 2 < CHUNKS:
            send_own(6 + 2 * c)
        land(2 + 2 * c)
        land_passed(2 + 2 * c)
        for m in order:
            row = plane_row(rank, m)
            project(
                active, w_down, all_mix, partial, m, row, row, rank, c * chunk, (c + 1) * chunk
            )
            combines[c].to_sibling(m)
        for m in order:
            combines[c].add_sibling(m)
        if c:
            for m in order:
                combines[c - 1].add_x(m)
        if c == 1:
            keep(w_gate_up, full_gate_up, 0)
            keep(all_mix, mix_out, 1)
    keep(w_down, full_down, 2)
    for m in order:
        combines[CHUNKS - 1].add_x(m)
    for one in combines:
        one.finish(inputs, out)
    for one in combines:
        one.drain()
    for copy in kept:
        copy.wait()
    for one in spreads:
        one.finish()
    for k in range(count):
        ways[k][0].wait_send()
        ways[k][1].wait_send()
        passes[k].wait_send()
    for copy in trades:
        copy.wait_recv()
    for copy in trades:
        copy.wait_send()


def bf16(*shape):
    return jax.ShapeDtypeStruct(shape, jnp.bfloat16)


def token_scratch(width, hidden_width, active_rows):
    return [
        pltpu.VMEM((2, width, hidden_width), jnp.bfloat16),
        pltpu.VMEM((hidden_width, width), jnp.bfloat16),
        pltpu.VMEM((active_rows, hidden_width), jnp.bfloat16),
        pltpu.VMEM((4, PLANE, width), jnp.bfloat16),
        pltpu.VMEM((4, 2, BLOCK, width), jnp.bfloat16),
        pltpu.VMEM((4, BLOCK, width), jnp.bfloat16),
        pltpu.VMEM((3, BLOCK, width), jnp.bfloat16),
    ]


def first_tick(inputs, gain, mix, gate_up, down, first, second):
    width, hidden_width = inputs.shape[1], gate_up.shape[2]
    rows = EXPERTS * BLOCK
    return pl.pallas_call(
        first_kernel,
        out_shape=(
            bf16(2, width, hidden_width), bf16(hidden_width, width),
            bf16(*gate_up.shape), bf16(*down.shape), bf16(*down.shape), bf16(*down.shape),
            jax.ShapeDtypeStruct((rows, 128), jnp.float32), bf16(*inputs.shape),
        ),
        in_specs=[VMEM] * 3 + [ANY] * 4,
        out_specs=[ANY] * 7 + [VMEM],
        scratch_shapes=[
            pltpu.VMEM((rows, width), jnp.bfloat16),
            pltpu.VMEM((rows, 128), jnp.float32),
            *token_scratch(width, hidden_width, rows),
            DMA((2 + 2 * CHUNKS, 3)), DMA((2 + 2 * CHUNKS, 3)), DMA((2 + 2 * CHUNKS,)), DMA((4,)), DMA((4,)),
            DMA((18,)), DMA((18,)), DMA((18,)), DMA((18,)), DMA((CHUNKS, 25)), DMA((CHUNKS, 25)),
        ],
        compiler_params=pltpu.CompilerParams(
            collective_id=0, has_side_effects=True, vmem_limit_bytes=60 << 20
        ),
        name="first_tick",
    )(inputs, gain, mix, gate_up, down, first, second)


def second_kernel(
    cut, inputs, gain, mix, full_gate_up, full_down, second, _, out, got_second,
    tokens, w_gate_up, w_down, active, partial, theirs, over_x, from_z, halves, last,
    here, trade_send, trade_recv, d_send, d_recv, c_send, c_recv,
):
    rank = lax.axis_index("expert")
    greet(group(rank))
    loads = []
    for i, (src, dst) in enumerate(((full_gate_up, w_gate_up), (full_down, w_down))):
        copy = pltpu.make_async_copy(src, dst, here.at[i])
        copy.start()
        loads.append(copy)
    spreads = []
    for i in range(2):
        norm_into(inputs, gain, tokens, rank, i * HALF, HALF)
        one = Spread(tokens, cut, (d_send.at[i], d_recv.at[i]), rank, i * HALF, HALF)
        one.begin()
        spreads.append(one)
    columns = (0, cut, inputs.shape[1])
    combine = Combine(partial, theirs, over_x, from_z, halves, last, columns, (c_send, c_recv), rank)

    def up(m):
        hidden(tokens, w_gate_up, active, plane_row(rank, m), 0)

    def project_out(m):
        project(active, w_down, mix, partial, m, plane_row(rank, m), 0, EXPERTS + rank, 0, inputs.shape[1])
        combine.to_sibling(m)

    def far(i):
        for one in spreads:
            one.forward_far_arrival(i)

    def wait_plane(i):
        for one in spreads:
            one.wait_plane(i)

    for one in spreads:
        one.forward_x_arrival()
        for i in range(3):
            one.forward_z_arrival(i)
    trade = remote(
        late(second), late(got_second), (trade_send.at[0], trade_recv.at[0]), {"expert": rank ^ 8}
    )
    trade.start()
    for copy in loads:
        copy.wait()
    for one in spreads:
        one.wait_own_plane()
    up(0)
    far(0)
    project_out(0)
    far(1)
    wait_plane(0)
    up(1)
    far(2)
    combine.add_sibling(0)
    project_out(1)
    wait_plane(1)
    up(2)
    combine.add_sibling(1)
    project_out(2)
    combine.add_x(0)
    wait_plane(2)
    up(3)
    combine.add_sibling(2)
    project_out(3)
    combine.add_x(1)
    combine.add_sibling(3)
    combine.add_x(2)
    combine.add_x(3)
    combine.finish(inputs, out)
    combine.drain()
    for one in spreads:
        one.finish()
    trade.wait_recv()
    trade.wait_send()


def second_tick(inputs, gain, mix, full_gate_up, full_down, second, got_second):
    width, hidden_width = inputs.shape[1], full_gate_up.shape[2]
    cut = 2560
    return pl.pallas_call(
        functools.partial(second_kernel, cut),
        out_shape=(bf16(*inputs.shape), bf16(*second.shape)),
        in_specs=[VMEM] * 3 + [ANY] * 4,
        out_specs=[VMEM, ANY],
        input_output_aliases={6: 1},
        scratch_shapes=[
            pltpu.VMEM((EXPERTS * BLOCK, width), jnp.bfloat16),
            *token_scratch(width, hidden_width, PLANE),
            pltpu.VMEM((3, 2, BLOCK, width - cut), jnp.bfloat16),
            pltpu.VMEM((BLOCK, width - cut), jnp.bfloat16),
            DMA((2,)), DMA((1,)), DMA((1,)), DMA((2, 18)), DMA((2, 18)), DMA((25,)), DMA((25,)),
        ],
        compiler_params=pltpu.CompilerParams(
            collective_id=1, has_side_effects=True, vmem_limit_bytes=60 << 20
        ),
        name="second_tick",
    )(inputs, gain, mix, full_gate_up, full_down, second, got_second)


def shifted(value, axis, distance):
    devices = range(lax.axis_size(axis))
    route = [(i - distance, i) for i in devices if i - distance in devices]
    return lax.ppermute(value, axis, route)


def per_device(
    fresh_tokens,
    in_flight,
    norm_weight,
    gate_up,
    down_proj,
    first_moment,
    second_moment,
    route_ids,
    route_probs,
    trade_flags,
):
    half_span = lax.axis_size("expert") // 2
    own_rank = lax.axis_index("expert")
    section_index = lax.axis_index("section")

    lanes = jnp.arange(128, dtype=jnp.int32)
    probs = route_probs[0]
    mix = probs / jnp.sum(probs, axis=-1, keepdims=True)
    wanted = route_ids[0] + EXPERTS * jnp.arange(2, dtype=jnp.int32)[:, None, None]
    dense_mix = jnp.sum(jnp.where(wanted[..., None] == lanes, mix[..., None], 0.0), axis=(0, 2))

    first_input = jnp.where(section_index == 0, fresh_tokens[0], in_flight)
    full_gate_up, full_down, *traded, all_mix, tick_zero = first_tick(
        first_input, norm_weight, dense_mix,
        gate_up[0, 0], down_proj[0, 0], first_moment[0, 0], second_moment[0, 0],
    )
    arrived = shifted(tick_zero, "section", 1)
    second_input = jnp.where(section_index == 0, fresh_tokens[1], arrived)
    tick_one, traded[3] = second_tick(
        second_input, norm_weight, all_mix, full_gate_up, full_down, second_moment[0, 0], traded[3]
    )
    layer_out = jnp.stack([tick_zero, tick_one])[None]

    moves = trade_flags[own_rank % half_span, 0] == 1
    kept = (gate_up, down_proj, first_moment, second_moment)
    moved = [
        jnp.where(moves, got.reshape(own.shape), own) for got, own in zip(traded, kept)
    ]
    return (layer_out, *moved)


def solution(mesh):
    return jax.shard_map(
        per_device,
        mesh=mesh,
        in_specs=(
            P(None, ("expert", "dp"), None),
            P(("expert", "dp"), None),
            P("section", None),
            P("section", "expert", None, "dp", None),
            P("section", "expert", "dp", None),
            P("section", "expert", "dp", None),
            P("section", "expert", "dp", None),
            P("section", None, ("expert", "dp"), None),
            P("section", None, ("expert", "dp"), None),
            P(),
        ),
        out_specs=(
            P("section", None, ("expert", "dp"), None),
            P("section", "expert", None, "dp", None),
            P("section", "expert", "dp", None),
            P("section", "expert", "dp", None),
            P("section", "expert", "dp", None),
        ),
        check_vma=False,
    )
```
